128 devices in a mesh: seq: 16 (over x, z), dp: 8 (over y, core).
Axes of the slice: x: 4, y: 4, z: 4, core: 2. Of those that a mesh axis runs over, the one named last changes fastest.
Arguments:
- layer_input: bfloat16 [8, 2048, 4096], P('dp', 'seq'), may hold values from -6 to 6
- query_rows: bfloat16 [8, 2048, 4096], P('dp', 'seq')
- key_rows: bfloat16 [8, 2048, 4096], P('dp', 'seq')
- value_rows: bfloat16 [8, 2048, 4096], P('dp', 'seq'), may hold values from -6 to 6
- out_grad: bfloat16 [8, 2048, 4096], P('dp', 'seq'), may hold values from -6 to 6
- neighbours: int32 [8, 16, 8], P('dp'), may hold values from 0 to 15, as said below
- counts: int32 [8, 16], P('dp'), may hold values from 1 to 8, as said below
Outputs:
- query_grad: bfloat16 [8, 2048, 4096], P('dp', 'seq')
- key_grad: bfloat16 [8, 2048, 4096], P('dp', 'seq')
- value_grad: bfloat16 [8, 2048, 4096], P('dp', 'seq')
- weight_grad: float32 [3, 4096, 4096], P(None, 'dp', 'seq')
The draws below stay inside these ranges and needn't reach their ends.
Inputs may be any that keep to these rules, and one draw needn't show every extreme that they name: `neighbours`: each row lists 8 distinct key blocks of the same snapshot, the query block itself first; entries past counts are not attended. `counts`: every snapshot has a query block with 8.
All inputs are finite; a program needn't handle non-finite values.
Results may differ from the reference program's by a relative error of at most 0.015.
Values may be sent and summed in bfloat16 or wider, within the bound.
A program may use at most 192 MiB of HBM per device.

```python
import jax
import jax.numpy as jnp
from jax import lax

D = 4096
H = 32
HDIM = 128
BLK = 128
MAXNB = 8
HD = 4096
SNAP_TOK = 2048
SNAPS = 8
NQB = 16
TOKENS = 16384


def shared_keys(key):
    return jax.random.normal(jax.random.fold_in(key, 31), (SNAPS, SNAP_TOK, HD), jnp.float32)


def draw_key_rows(key, part):
    key_base = shared_keys(key)
    return key_base.astype(jnp.bfloat16)


def draw_query_rows(key, part):
    queries = jax.random.normal(jax.random.fold_in(key, 41), (SNAPS, SNAP_TOK, HD), jnp.float32)
    return queries.astype(jnp.bfloat16)


def draw_neighbours(key, part):
    random_part = jax.random.randint(jax.random.fold_in(key, 23), (SNAPS, NQB, NQB), 0, NQB)
    index = jnp.arange(NQB)
    distance = jnp.abs(index[None, None, :] - index[None, :, None])
    ranking = (random_part + 2 * distance) * NQB + index[None, None, :]
    ranking = jnp.where(index[None, None, :] == index[None, :, None], -1, ranking)
    order = jnp.argsort(ranking, axis=-1, stable=True)
    return order[:, :, :MAXNB].astype(jnp.int32)


def draw_counts(key, part):
    ceiling = jax.random.randint(jax.random.fold_in(key, 11), (SNAPS, 1), 2, MAXNB + 1)
    base = jax.random.randint(jax.random.fold_in(key, 13), (SNAPS, NQB), 0, 1 << 20) % ceiling + 1
    fullest = jax.random.randint(jax.random.fold_in(key, 17), (SNAPS, 1), 0, NQB)
    base = jnp.where(jnp.arange(NQB)[None, :] == fullest, MAXNB, base)
    return base.astype(jnp.int32)


def block_scale(rng, extent, cuts, smallest, largest):
    loudness = 1.0
    for axis_at, shards_of in cuts:
        heights = jax.random.uniform(jax.random.fold_in(jax.random.fold_in(rng, 6), axis_at), (shards_of,), jnp.float32, smallest / len(cuts), largest / len(cuts))
        loudness = loudness * jnp.repeat(jnp.exp(heights), extent[axis_at] // shards_of).reshape((-1,) + (1,) * (len(extent) - 1 - axis_at))
    return loudness


def scatter_about(stream_key, extent, width, limit, cuts=(), kind=jnp.bfloat16):
    values = jax.random.normal(stream_key, extent, jnp.float32) * width
    if len(cuts) > 0:
        values = block_scale(stream_key, extent, cuts, -0.22, 0.18) * values
    return jnp.clip(values, min=-limit, max=limit).astype(kind)


def setup_inputs(seed: int = 0) -> dict:
    key_of = jax.random.split(jax.random.key(seed), 8)
    return {
        "layer_input": scatter_about(key_of[0], (SNAPS, SNAP_TOK, D), 1.0, 6.0, ((0, 8), (1, 16))),
        "query_rows": draw_query_rows(jax.random.fold_in(key_of[7], 71), 0),
        "key_rows": draw_key_rows(jax.random.fold_in(key_of[7], 71), 0),
        "value_rows": scatter_about(key_of[3], (SNAPS, SNAP_TOK, HD), 1.0, 6.0, ((0, 8), (1, 16))),
        "out_grad": scatter_about(key_of[4], (SNAPS, SNAP_TOK, HD), 1.0, 6.0, ((0, 8), (1, 16))),
        "neighbours": draw_neighbours(jax.random.fold_in(key_of[7], 71), 0),
        "counts": draw_counts(jax.random.fold_in(key_of[7], 71), 0),
    }


def block_backward(query_head, key_head, value_head, grad_head, links, tallies):
    score_scale = HDIM ** -0.5
    query_blocks = query_head.reshape(NQB, BLK, HDIM).astype(jnp.float32)
    key_near = key_head.reshape(NQB, BLK, HDIM)[links].reshape(NQB, MAXNB * BLK, HDIM).astype(jnp.float32)
    value_near = value_head.reshape(NQB, BLK, HDIM)[links].reshape(NQB, MAXNB * BLK, HDIM).astype(jnp.float32)
    grad_blocks = grad_head.reshape(NQB, BLK, HDIM).astype(jnp.float32)
    live_slot = jnp.arange(MAXNB)[None, :] < tallies[:, None]
    live_keys = jnp.repeat(live_slot, BLK, axis=1)[:, None, :]
    scores = jnp.einsum("qtd,qkd->qtk", query_blocks, key_near) * score_scale
    scores = jnp.where(live_keys, scores, -jnp.inf)
    top_score = jnp.max(scores, axis=-1, keepdims=True)
    weights = jnp.exp(scores - top_score)
    probs = weights / jnp.sum(weights, axis=-1, keepdims=True)
    probs_low = lax.optimization_barrier(probs.astype(jnp.bfloat16)).astype(jnp.float32)
    value_part = jnp.einsum("qtk,qtd->qkd", probs_low, grad_blocks)
    prob_grad = jnp.einsum("qtd,qkd->qtk", grad_blocks, value_near)
    row_dot = jnp.sum(probs * prob_grad, axis=-1, keepdims=True)
    score_grad = lax.optimization_barrier((probs * (prob_grad - row_dot) * score_scale).astype(jnp.bfloat16)).astype(jnp.float32)
    query_part = jnp.einsum("qtk,qkd->qtd", score_grad, key_near)
    key_part = jnp.einsum("qtk,qtd->qkd", score_grad, query_blocks)
    flat_links = links.reshape(-1)
    key_sum = jnp.zeros((NQB, BLK, HDIM), jnp.float32).at[flat_links].add(key_part.reshape(NQB * MAXNB, BLK, HDIM))
    value_sum = jnp.zeros((NQB, BLK, HDIM), jnp.float32).at[flat_links].add(value_part.reshape(NQB * MAXNB, BLK, HDIM))
    return query_part.reshape(SNAP_TOK, HDIM), key_sum.reshape(SNAP_TOK, HDIM), value_sum.reshape(SNAP_TOK, HDIM)


def split_heads(array):
    return array.reshape(SNAP_TOK, H, HDIM).transpose(1, 0, 2)


def join_heads(array):
    return array.transpose(1, 0, 2).reshape(SNAP_TOK, HD).astype(jnp.bfloat16)


def snapshot_backward(snap_items):
    query_snap, key_snap, value_snap, grad_snap, links, tallies = snap_items

    def one_head(head_items):
        return block_backward(head_items[0], head_items[1], head_items[2], head_items[3], links, tallies)

    results = lax.map(one_head, (split_heads(query_snap), split_heads(key_snap), split_heads(value_snap), split_heads(grad_snap)))
    return join_heads(results[0]), join_heads(results[1]), join_heads(results[2])


def reference(layer_input, query_rows, key_rows, value_rows, out_grad, neighbours, counts):
    query_grad, key_grad, value_grad = lax.map(snapshot_backward, (query_rows, key_rows, value_rows, out_grad, neighbours, counts))
    pieces = []
    for grads in (query_grad, key_grad, value_grad):
        total = jnp.zeros((D, HD), jnp.float32)
        for snap in range(SNAPS):
            partial_sum = jnp.dot(layer_input[snap].T, grads[snap], preferred_element_type=jnp.float32)
            total = total + lax.optimization_barrier(partial_sum.astype(jnp.bfloat16)).astype(jnp.float32)
        pieces.append(total)
    weight_grad = jnp.stack(pieces, axis=0) * (1.0 / (TOKENS ** 0.5))
    return query_grad, key_grad, value_grad, weight_grad
```

```python
import functools
import math

import jax
import jax.numpy as jnp
from jax import lax
from jax.experimental import pallas as pl
from jax.experimental.pallas import tpu as pltpu
from jax.sharding import PartitionSpec as P

HDIM = 128
BLK = 128
MAXNB = 8
NQB = 16
SEQ = 16
SIDE = 4
COLS = 256
MESH = pl.DeviceIdType.MESH


def offsets():
    pairs = [(dx, dz) for dx in range(SIDE) for dz in range(SIDE) if dx or dz]
    far = lambda d: min(d, SIDE - d)
    return sorted(pairs, key=lambda p: -(far(p[0]) + far(p[1])))


def peer_of(me, dx, dz):
    x, z = me // SIDE, lax.rem(me, SIDE)
    return lax.rem(x + dx, SIDE) * SIDE + lax.rem(z + dz, SIDE)


def greet(me):
    barrier = pltpu.get_barrier_semaphore()
    for dx, dz in offsets():
        pl.semaphore_signal(
            barrier, inc=1, device_id={"seq": peer_of(me, dx, dz)}, device_id_type=MESH
        )
    pl.semaphore_wait(barrier, SEQ - 1)


def to_heads_kernel(count, *refs):
    ins, outs = refs[:count], refs[count : 2 * count]
    send_sem, recv_sem, own_sem = refs[2 * count :]
    me = lax.axis_index("seq")
    greet(me)
    rows = pl.ds(pl.multiple_of(me * BLK, BLK), BLK)
    copies = []
    for i, (dx, dz) in enumerate(offsets()):
        peer = peer_of(me, dx, dz)
        cols = pl.ds(pl.multiple_of(peer * COLS, COLS), COLS)
        for a in range(count):
            copy = pltpu.make_async_remote_copy(
                src_ref=ins[a].at[:, cols],
                dst_ref=outs[a].at[rows, :],
                send_sem=send_sem.at[a, i],
                recv_sem=recv_sem.at[a, i],
                device_id={"seq": peer},
                device_id_type=MESH,
            )
            copy.start()
            copies.append(copy)
    mine = pl.ds(pl.multiple_of(me * COLS, COLS), COLS)
    for a in range(count):
        own = pltpu.make_async_copy(ins[a].at[:, mine], outs[a].at[rows, :], own_sem.at[a])
        own.start()
        copies.append(own)
    for copy in copies:
        copy.wait()


def to_rows_kernel(count, *refs):
    ins, outs = refs[:count], refs[count : 2 * count]
    send_sem, recv_sem, own_sem = refs[2 * count :]
    me = lax.axis_index("seq")
    greet(me)
    mine = pl.ds(pl.multiple_of(me * COLS, COLS), COLS)
    copies = []
    for i, (dx, dz) in enumerate(offsets()):
        peer = peer_of(me, dx, dz)
        rows = pl.ds(pl.multiple_of(peer * BLK, BLK), BLK)
        for a in range(count):
            copy = pltpu.make_async_remote_copy(
                src_ref=ins[a].at[rows, :],
                dst_ref=outs[a].at[:, mine],
                send_sem=send_sem.at[a, i],
                recv_sem=recv_sem.at[a, i],
                device_id={"seq": peer},
                device_id_type=MESH,
            )
            copy.start()
            copies.append(copy)
    rows = pl.ds(pl.multiple_of(me * BLK, BLK), BLK)
    for a in range(count):
        own = pltpu.make_async_copy(ins[a].at[rows, :], outs[a].at[:, mine], own_sem.at[a])
        own.start()
        copies.append(own)
    for copy in copies:
        copy.wait()


def exchange(kernel, arrays, shape, collective_id):
    count = len(arrays)
    moved = count * SEQ * BLK * COLS * 2
    return pl.pallas_call(
        functools.partial(kernel, count),
        out_shape=[jax.ShapeDtypeStruct(shape, jnp.bfloat16)] * count,
        in_specs=[pl.BlockSpec(memory_space=pl.ANY)] * count,
        out_specs=[pl.BlockSpec(memory_space=pl.ANY)] * count,
        scratch_shapes=[
            pltpu.SemaphoreType.DMA((count, SEQ - 1)),
            pltpu.SemaphoreType.DMA((count, SEQ - 1)),
            pltpu.SemaphoreType.DMA((count,)),
        ],
        compiler_params=pltpu.CompilerParams(
            collective_id=collective_id, has_side_effects=True
        ),
        cost_estimate=pl.CostEstimate(flops=0, bytes_accessed=16 * moved, transcendentals=0),
    )(*arrays)


def attend(kv_links, tallies, q_ref, k_ref, v_ref, g_ref, dq_ref, dk_ref, dv_ref, wq, turned, acc, sp):
    scale = HDIM ** (-0.5)
    heads = COLS // HDIM
    f32 = jnp.float32
    acc[...] = jnp.zeros_like(acc)
    wq[...] = jnp.zeros_like(wq)

    @pl.loop(0, NQB)
    def _(n):
        rows = pl.ds(pl.multiple_of(n * BLK, BLK), BLK)
        for h in range(heads):
            turned[h, n] = k_ref[rows, h * HDIM : (h + 1) * HDIM].astype(f32).T.astype(jnp.bfloat16)

    @pl.loop(0, NQB)
    def _(b):
        mine = pl.ds(pl.multiple_of(b * BLK, BLK), BLK)
        tally = tallies[b]

        def variant(slots):
            for h in range(heads):
                cols = slice(h * HDIM, (h + 1) * HDIM)
                wq[h, :HDIM, :HDIM] = q_ref[mine, cols]
                wq[h, HDIM:, HDIM:] = g_ref[mine, cols]
            for h in range(heads):
                cols = slice(h * HDIM, (h + 1) * HDIM)
                both = wq[h]
                top = None
                for j in range(slots):
                    rows = pl.ds(pl.multiple_of(kv_links[b, j] * BLK, BLK), BLK)
                    kv = jnp.concatenate([k_ref[rows, cols], v_ref[rows, cols]], axis=1)
                    pair = lax.dot_general(
                        kv, both, (((1,), (1,)), ((), ())), preferred_element_type=f32
                    )
                    score = pair[:, :HDIM]
                    if j == slots - 1 and slots > 1:
                        score = jnp.where(j < tally, score, -jnp.inf)
                    sp[h, j, :, :HDIM] = score
                    sp[h, j, :, HDIM:] = pair[:, HDIM:]
                    here = jnp.max(score, axis=0, keepdims=True)
                    top = here if top is None else jnp.maximum(top, here)
                total = jnp.zeros((1, HDIM), f32)
                dot = jnp.zeros((1, HDIM), f32)
                for j in range(slots):
                    weight = jnp.exp((sp[h, j, :, :HDIM] - top) * scale)
                    sp[h, j, :, :HDIM] = weight
                    total += jnp.sum(weight, axis=0, keepdims=True)
                    dot += jnp.sum(weight * sp[h, j, :, HDIM:], axis=0, keepdims=True)
                inverse = 1.0 / total
                dot = dot * inverse
                dq = jnp.zeros((HDIM, BLK), f32)
                for j in range(slots):
                    link = kv_links[b, j]
                    rows = pl.ds(pl.multiple_of(link * BLK, BLK), BLK)
                    prob = sp[h, j, :, :HDIM] * inverse
                    slope = (prob * (sp[h, j, :, HDIM:] - dot) * scale).astype(jnp.bfloat16)
                    left = jnp.concatenate([slope, prob.astype(jnp.bfloat16)], axis=1)
                    acc[h, rows, :] += jnp.dot(left, both, preferred_element_type=f32)
                    dq += jnp.dot(turned[h, link], slope, preferred_element_type=f32)
                dq_ref[mine, cols] = dq.T.astype(jnp.bfloat16)

        for slots in range(2, MAXNB + 1, 2):
            pl.when((tally == slots) | (tally == slots - 1))(functools.partial(variant, slots))

    @pl.loop(0, NQB)
    def _(n):
        rows = pl.ds(pl.multiple_of(n * BLK, BLK), BLK)
        for h in range(heads):
            cols = slice(h * HDIM, (h + 1) * HDIM)
            dk_ref[rows, cols] = acc[h, rows, :HDIM].astype(jnp.bfloat16)
            dv_ref[rows, cols] = acc[h, rows, HDIM:].astype(jnp.bfloat16)


def attention(links, tallies, q, k, v, g):
    tokens = NQB * BLK
    heads = COLS // HDIM
    spec = pl.BlockSpec(memory_space=pltpu.VMEM)
    smem = pl.BlockSpec(memory_space=pltpu.SMEM)
    flops = heads * NQB * MAXNB * 5 * 2 * BLK**3
    return pl.pallas_call(
        attend,
        out_shape=[jax.ShapeDtypeStruct((tokens, COLS), jnp.bfloat16)] * 3,
        in_specs=[smem, smem] + [spec] * 4,
        out_specs=[spec] * 3,
        scratch_shapes=[
            pltpu.VMEM((heads, 2 * HDIM, 2 * BLK), jnp.bfloat16),
            pltpu.VMEM((heads, NQB, HDIM, BLK), jnp.bfloat16),
            pltpu.VMEM((heads, tokens, 2 * HDIM), jnp.float32),
            pltpu.VMEM((heads, MAXNB, BLK, 2 * BLK), jnp.float32),
        ],
        compiler_params=pltpu.CompilerParams(vmem_limit_bytes=40 << 20),
        cost_estimate=pl.CostEstimate(
            flops=flops, bytes_accessed=7 * tokens * COLS * 2, transcendentals=heads * NQB * MAXNB * BLK * BLK
        ),
    )(links, tallies, q, k, v, g)


def local(layer_input, query_rows, key_rows, value_rows, out_grad, neighbours, counts):
    dp_count = lax.axis_size("dp")
    tokens = NQB * BLK
    q, k, v, g = exchange(
        to_heads_kernel,
        [query_rows[0], key_rows[0], value_rows[0], out_grad[0]],
        (tokens, COLS),
        0,
    )
    whole = lax.all_gather(layer_input, "seq", axis=1, tiled=True)
    dq, dk, dv = attention(neighbours[0], counts[0], q, k, v, g)
    width = query_rows.shape[2]
    query_grad, key_grad, value_grad = exchange(
        to_rows_kernel, [dq, dk, dv], (BLK, width), 1
    )
    terms = [
        jnp.dot(whole[0].T, part, preferred_element_type=jnp.float32) for part in (dq, dk, dv)
    ]
    summed = jnp.stack(terms, axis=0).astype(jnp.bfloat16)
    owned = lax.psum_scatter(summed, "dp", scatter_dimension=1, tiled=True).astype(jnp.float32)
    norm_factor = 1.0 / math.sqrt(tokens * dp_count)
    return query_grad[None], key_grad[None], value_grad[None], owned * norm_factor


def solution(mesh):
    rows = P("dp", "seq", None)
    return jax.shard_map(
        local,
        mesh=mesh,
        in_specs=(rows,) * 5 + (P("dp", None, None), P("dp", None)),
        out_specs=(rows, rows, rows, P(None, "dp", "seq")),
        check_vma=False,
    )
```

```python
import functools
import math

import jax
import jax.numpy as jnp
from jax import lax
from jax.experimental import pallas as pl
from jax.experimental.pallas import tpu as pltpu
from jax.sharding import PartitionSpec as P

HDIM = 128
BLK = 128
MAXNB = 8
NQB = 16
SEQ = 16
SIDE = 4
COLS = 256
MESH = pl.DeviceIdType.MESH


OFFSETS = (
    (2, 2), (2, 1), (2, 3), (1, 2), (3, 2), (2, 0), (0, 2), (1, 1),
    (3, 3), (1, 3), (3, 1), (1, 0), (3, 0), (0, 1), (0, 3),
)


def peer_of(offset):
    me, core = lax.axis_index("seq"), lax.rem(lax.axis_index("dp"), 2)
    place = []
    for at, step in zip((me // SIDE, lax.rem(me, SIDE)), offset):
        back = (SIDE - step) % SIDE
        place.append(lax.rem(at + step + core * (back - step), SIDE))
    return place[0] * SIDE + place[1]


def block(index, size):
    return pl.ds(pl.multiple_of(index * size, size), size)


def to_heads(*refs):
    ins, outs = refs[:4], refs[4:8]
    send_sem, recv_sem, own_sem = refs[8:]
    me = lax.axis_index("seq")
    barrier = pltpu.get_barrier_semaphore()
    for offset in OFFSETS:
        pl.semaphore_signal(
            barrier, inc=1, device_id={"seq": peer_of(offset)}, device_id_type=MESH
        )
    pl.semaphore_wait(barrier, SEQ - 1)
    copies = []
    for a in range(4):
        for i, offset in enumerate(OFFSETS):
            peer = peer_of(offset)
            copy = pltpu.make_async_remote_copy(
                src_ref=ins[a].at[:, block(peer, COLS)],
                dst_ref=outs[a].at[block(me, BLK), :],
                send_sem=send_sem.at[a, i],
                recv_sem=recv_sem.at[a, i],
                device_id={"seq": peer},
                device_id_type=MESH,
            )
            copy.start()
            copies.append(copy)
    for a in range(4):
        own = pltpu.make_async_copy(
            ins[a].at[:, block(me, COLS)], outs[a].at[block(me, BLK), :], own_sem.at[a]
        )
        own.start()
        copies.append(own)
    for copy in copies:
        copy.wait()


def heads_exchange(arrays):
    tokens = SEQ * BLK
    return pl.pallas_call(
        to_heads,
        out_shape=[jax.ShapeDtypeStruct((tokens, COLS), jnp.bfloat16)] * 4,
        in_specs=[pl.BlockSpec(memory_space=pl.ANY)] * 4,
        out_specs=[pl.BlockSpec(memory_space=pltpu.VMEM)] * 4,
        scratch_shapes=[
            pltpu.SemaphoreType.DMA((4, SEQ - 1)),
            pltpu.SemaphoreType.DMA((4, SEQ - 1)),
            pltpu.SemaphoreType.DMA((4,)),
        ],
        compiler_params=pltpu.CompilerParams(
            collective_id=0, has_side_effects=True, vmem_limit_bytes=16 << 20
        ),
    )(*arrays)


STRIPS = 4
STRIP = 1024
TURNS = (2, 1, 3, 0)
WIDE = 3 * COLS
PIECE = 512


def finish(x_ref, dq_ref, dk_ref, dv_ref, qg_ref, kg_ref, vg_ref, w_ref,
           xg, gt, keep, sib_out, sib_in, y_out, y_in,
           load_sem, ring_send, ring_recv, back_send, back_recv, own_sem, sib_sem, y_sem):
    me, dp = lax.axis_index("seq"), lax.axis_index("dp")
    x, z, y, core = me // SIDE, lax.rem(me, SIDE), dp // 2, lax.rem(dp, 2)
    turn = lambda at, by: lax.rem(at + by, SIDE)
    f32 = jnp.float32
    grads, homes = (dq_ref, dk_ref, dv_ref), (qg_ref, kg_ref, vg_ref)

    loads = []
    for k in range(STRIPS):
        load = pltpu.make_async_copy(
            x_ref.at[:, block(turn(y, TURNS[k]), STRIP)], xg.at[k, x, z], load_sem.at[k]
        )
        load.start()
        loads.append(load)
    barrier = pltpu.get_barrier_semaphore()
    friends = [(peer_of(offset), dp) for offset in OFFSETS]
    friends += [(me, y * 2 + 1 - core)]
    friends += [(me, turn(y, by) * 2 + core) for by in (1, 2, 3)]
    for friend in friends:
        pl.semaphore_signal(barrier, inc=1, device_id=friend, device_id_type=MESH)
    pl.semaphore_wait(barrier, len(friends))

    started = []

    def send(src, dst, sems, device):
        copy = pltpu.make_async_remote_copy(
            src_ref=src, dst_ref=dst, send_sem=sems[0], recv_sem=sems[1],
            device_id=device, device_id_type=MESH,
        )
        copy.start()
        started.append(copy)
        return copy

    def ring(k, part, stage):
        cols = slice(part * (STRIP // 2), (part + 1) * (STRIP // 2))
        along_x = (part == 0) == (stage < 2)
        copies = []
        for way, step in enumerate((1, 3)):
            owner = 0 if stage % 2 == 0 else SIDE - step
            rows = slice(0, BLK) if stage % 2 == 0 else slice(way * (BLK // 2), (way + 1) * (BLK // 2))
            if along_x:
                device = (turn(x, step) * SIDE + z, dp)
                group = (turn(x, owner), z if stage < 2 else slice(None))
            else:
                device = (x * SIDE + turn(z, step), dp)
                group = (x if stage < 2 else slice(None), turn(z, owner))
            place = xg.at[k, group[0], group[1], rows, cols]
            at = ((k * 2 + part) * 4 + stage) * 2 + way
            copies.append(send(place, place, (ring_send.at[at], ring_recv.at[at]), device))
        return copies

    flights = {}

    def advance(k, stage):
        for part in (0, 1):
            if stage == 0 and part == 0:
                loads[k].wait()
            if stage > 0:
                for copy in flights[k, part, stage - 1]:
                    copy.wait_recv()
            if stage < 4:
                flights[k, part, stage] = ring(k, part, stage)

    homeward = []

    def go_home(a):
        for i, offset in enumerate(OFFSETS):
            peer = peer_of(offset)
            homeward.append(send(
                grads[a].at[block(peer, BLK), :], homes[a].at[:, block(me, COLS)],
                (back_send.at[a, i], back_recv.at[a, i]), (peer, dp),
            ))
        own = pltpu.make_async_copy(
            grads[a].at[block(me, BLK), :], homes[a].at[:, block(me, COLS)], own_sem.at[a]
        )
        own.start()
        owns.append(own)

    owns, siblings, across = [], [], []

    def product(k):
        for half in (0, 1):
            first = (1 - core if half == 0 else core) * PIECE

            @pl.loop(0, PIECE // 256)
            def _(tile):
                cols = pl.ds(pl.multiple_of(first + tile * 256, 256), 256)
                here = pl.ds(pl.multiple_of(tile * 256, 256), 256)
                right = xg[k, :, :, :, cols].reshape(SEQ * BLK, 256)
                value = jnp.dot(gt[...], right, preferred_element_type=f32)
                if half == 0:
                    sib_out[k, :, here] = value.astype(jnp.bfloat16)
                else:
                    keep[k % 2, :, here] = value

            if half == 0:
                siblings.append(send(
                    sib_out.at[k], sib_in.at[k], (sib_sem.at[0, k], sib_sem.at[1, k]),
                    (me, y * 2 + 1 - core),
                ))

    def settle(k):
        siblings[k].wait_recv()
        if k < STRIPS - 1:
            y_out[k] = (keep[k % 2] + sib_in[k].astype(f32)).astype(jnp.bfloat16)
            across.append(send(
                y_out.at[k], y_in.at[k], (y_sem.at[0, k], y_sem.at[1, k]),
                (me, turn(y, TURNS[k]) * 2 + core),
            ))
        else:
            total = keep[k % 2] + sib_in[k].astype(f32)
            for i, copy in enumerate(across):
                copy.wait_recv()
                total += y_in[i].astype(f32)
            w_ref[...] = total

    for k in range(STRIPS):
        advance(k, 0)
    go_home(0)
    for k in range(STRIPS):
        advance(k, 1)
    advance(0, 2)
    advance(1, 2)

    @pl.loop(0, SEQ)
    def _(n):
        for a in range(3):
            for h in range(2):
                tile = grads[a][block(n, BLK), h * HDIM : (h + 1) * HDIM]
                gt[a * COLS + h * HDIM : a * COLS + (h + 1) * HDIM, block(n, BLK)] = tile.T

    for k in range(STRIPS):
        advance(k, 3)
        if k + 2 < STRIPS:
            advance(k + 2, 2)
        if k < 2:
            go_home(k + 1)
        if k >= 1:
            advance(k - 1, 4)
            product(k - 1)
        if k >= 2:
            settle(k - 2)
    settle(STRIPS - 2)
    advance(STRIPS - 1, 4)
    product(STRIPS - 1)
    settle(STRIPS - 1)
    for copy in homeward:
        copy.wait_recv()
    for own in owns:
        own.wait()
    for copy in started:
        copy.wait_send()


def closing(layer_rows, dq, dk, dv):
    tokens, width = SEQ * BLK, layer_rows.shape[1]
    vmem, any_place = pl.BlockSpec(memory_space=pltpu.VMEM), pl.BlockSpec(memory_space=pl.ANY)
    bf16, f32 = jnp.bfloat16, jnp.float32
    rings = STRIPS * 16
    return pl.pallas_call(
        finish,
        out_shape=[jax.ShapeDtypeStruct((BLK, width), bf16)] * 3
        + [jax.ShapeDtypeStruct((WIDE, PIECE), f32)],
        in_specs=[any_place, vmem, vmem, vmem],
        out_specs=[any_place] * 3 + [vmem],
        scratch_shapes=[
            pltpu.VMEM((STRIPS, SIDE, SIDE, BLK, STRIP), bf16),
            pltpu.VMEM((WIDE, tokens), bf16),
            pltpu.VMEM((2, WIDE, PIECE), f32),
            pltpu.VMEM((STRIPS, WIDE, PIECE), bf16),
            pltpu.VMEM((STRIPS, WIDE, PIECE), bf16),
            pltpu.VMEM((STRIPS - 1, WIDE, PIECE), bf16),
            pltpu.VMEM((STRIPS - 1, WIDE, PIECE), bf16),
            pltpu.SemaphoreType.DMA((STRIPS,)),
            pltpu.SemaphoreType.DMA((rings,)),
            pltpu.SemaphoreType.DMA((rings,)),
            pltpu.SemaphoreType.DMA((3, SEQ - 1)),
            pltpu.SemaphoreType.DMA((3, SEQ - 1)),
            pltpu.SemaphoreType.DMA((3,)),
            pltpu.SemaphoreType.DMA((2, STRIPS)),
            pltpu.SemaphoreType.DMA((2, STRIPS - 1)),
        ],
        compiler_params=pltpu.CompilerParams(
            collective_id=1, has_side_effects=True, vmem_limit_bytes=56 << 20
        ),
    )(layer_rows, dq, dk, dv)


def attend(kv_links, tallies, q_ref, k_ref, v_ref, g_ref, dq_ref, dk_ref, dv_ref, wq, turned, acc, sp):
    scale = HDIM ** (-0.5)
    heads = COLS // HDIM
    f32 = jnp.float32
    acc[...] = jnp.zeros_like(acc)
    wq[...] = jnp.zeros_like(wq)

    @pl.loop(0, NQB)
    def _(n):
        rows = pl.ds(pl.multiple_of(n * BLK, BLK), BLK)
        for h in range(heads):
            turned[h, n] = k_ref[rows, h * HDIM : (h + 1) * HDIM].astype(f32).T.astype(jnp.bfloat16)

    @pl.loop(0, NQB)
    def _(b):
        mine = pl.ds(pl.multiple_of(b * BLK, BLK), BLK)
        tally = tallies[b]

        def variant(slots):
            for h in range(heads):
                cols = slice(h * HDIM, (h + 1) * HDIM)
                wq[h, :HDIM, :HDIM] = q_ref[mine, cols]
                wq[h, HDIM:, HDIM:] = g_ref[mine, cols]
            for h in range(heads):
                cols = slice(h * HDIM, (h + 1) * HDIM)
                both = wq[h]
                top = None
                for j in range(slots):
                    rows = pl.ds(pl.multiple_of(kv_links[b, j] * BLK, BLK), BLK)
                    kv = jnp.concatenate([k_ref[rows, cols], v_ref[rows, cols]], axis=1)
                    pair = lax.dot_general(
                        kv, both, (((1,), (1,)), ((), ())), preferred_element_type=f32
                    )
                    score = pair[:, :HDIM]
                    if j == slots - 1 and slots > 1:
                        score = jnp.where(j < tally, score, -jnp.inf)
                    sp[h, j, :, :HDIM] = score
                    sp[h, j, :, HDIM:] = pair[:, HDIM:]
                    here = jnp.max(score, axis=0, keepdims=True)
                    top = here if top is None else jnp.maximum(top, here)
                total = jnp.zeros((1, HDIM), f32)
                dot = jnp.zeros((1, HDIM), f32)
                for j in range(slots):
                    weight = jnp.exp((sp[h, j, :, :HDIM] - top) * scale)
                    sp[h, j, :, :HDIM] = weight
                    total += jnp.sum(weight, axis=0, keepdims=True)
                    dot += jnp.sum(weight * sp[h, j, :, HDIM:], axis=0, keepdims=True)
                inverse = 1.0 / total
                dot = dot * inverse
                dq = jnp.zeros((HDIM, BLK), f32)
                for j in range(slots):
                    link = kv_links[b, j]
                    rows = pl.ds(pl.multiple_of(link * BLK, BLK), BLK)
                    prob = sp[h, j, :, :HDIM] * inverse
                    slope = (prob * (sp[h, j, :, HDIM:] - dot) * scale).astype(jnp.bfloat16)
                    left = jnp.concatenate([slope, prob.astype(jnp.bfloat16)], axis=1)
                    acc[h, rows, :] += jnp.dot(left, both, preferred_element_type=f32)
                    dq += jnp.dot(turned[h, link], slope, preferred_element_type=f32)
                dq_ref[mine, cols] = dq.T.astype(jnp.bfloat16)

        for slots in range(2, MAXNB + 1, 2):
            pl.when((tally == slots) | (tally == slots - 1))(functools.partial(variant, slots))

    @pl.loop(0, NQB)
    def _(n):
        rows = pl.ds(pl.multiple_of(n * BLK, BLK), BLK)
        for h in range(heads):
            cols = slice(h * HDIM, (h + 1) * HDIM)
            dk_ref[rows, cols] = acc[h, rows, :HDIM].astype(jnp.bfloat16)
            dv_ref[rows, cols] = acc[h, rows, HDIM:].astype(jnp.bfloat16)


def attention(links, tallies, q, k, v, g):
    tokens = NQB * BLK
    heads = COLS // HDIM
    spec = pl.BlockSpec(memory_space=pltpu.VMEM)
    smem = pl.BlockSpec(memory_space=pltpu.SMEM)
    flops = heads * NQB * MAXNB * 5 * 2 * BLK**3
    return pl.pallas_call(
        attend,
        out_shape=[jax.ShapeDtypeStruct((tokens, COLS), jnp.bfloat16)] * 3,
        in_specs=[smem, smem] + [spec] * 4,
        out_specs=[spec] * 3,
        scratch_shapes=[
            pltpu.VMEM((heads, 2 * HDIM, 2 * BLK), jnp.bfloat16),
            pltpu.VMEM((heads, NQB, HDIM, BLK), jnp.bfloat16),
            pltpu.VMEM((heads, tokens, 2 * HDIM), jnp.float32),
            pltpu.VMEM((heads, MAXNB, BLK, 2 * BLK), jnp.float32),
        ],
        compiler_params=pltpu.CompilerParams(vmem_limit_bytes=40 << 20),
        cost_estimate=pl.CostEstimate(
            flops=flops, bytes_accessed=7 * tokens * COLS * 2, transcendentals=heads * NQB * MAXNB * BLK * BLK
        ),
    )(links, tallies, q, k, v, g)


def local(layer_input, query_rows, key_rows, value_rows, out_grad, neighbours, counts):
    q, k, v, g = heads_exchange([query_rows[0], key_rows[0], value_rows[0], out_grad[0]])
    dq, dk, dv = attention(neighbours[0], counts[0], q, k, v, g)
    query_grad, key_grad, value_grad, turned = closing(layer_input[0], dq, dk, dv)
    norm_factor = 1.0 / math.sqrt(SEQ * BLK * lax.axis_size("dp"))
    owned = turned.reshape(3, COLS, PIECE).transpose(0, 2, 1) * norm_factor
    return query_grad[None], key_grad[None], value_grad[None], owned


def solution(mesh):
    rows = P("dp", "seq", None)
    return jax.shard_map(
        local,
        mesh=mesh,
        in_specs=(rows,) * 5 + (P("dp", None, None), P("dp", None)),
        out_specs=(rows, rows, rows, P(None, "dp", "seq")),
        check_vma=False,
    )
```

```python
import functools
import math

import jax
import jax.numpy as jnp
from jax import lax
from jax.experimental import pallas as pl
from jax.experimental.pallas import tpu as pltpu
from jax.sharding import PartitionSpec as P

HDIM = 128
BLK = 128
MAXNB = 8
NQB = 16
SEQ = 16
SIDE = 4
COLS = 256
LOG2E = 1.4426950408889634
MESH = pl.DeviceIdType.MESH


OFFSETS = (
    (2, 2), (2, 1), (2, 3), (1, 2), (3, 2), (2, 0), (0, 2), (1, 1),
    (3, 3), (1, 3), (3, 1), (1, 0), (3, 0), (0, 1), (0, 3),
)


def peer_of(offset):
    me, core = lax.axis_index("seq"), lax.rem(lax.axis_index("dp"), 2)
    place = []
    for at, step in zip((me // SIDE, lax.rem(me, SIDE)), offset):
        back = (SIDE - step) % SIDE
        place.append(lax.rem(at + step + core * (back - step), SIDE))
    return place[0] * SIDE + place[1]


def block(index, size):
    return pl.ds(pl.multiple_of(index * size, size), size)


def to_heads(*refs):
    ins, outs = refs[:4], refs[4:8]
    send_sem, recv_sem, own_sem = refs[8:]
    me = lax.axis_index("seq")
    barrier = pltpu.get_barrier_semaphore()
    for offset in OFFSETS:
        pl.semaphore_signal(
            barrier, inc=1, device_id={"seq": peer_of(offset)}, device_id_type=MESH
        )
    pl.semaphore_wait(barrier, SEQ - 1)
    copies = []
    for a in range(4):
        for i, offset in enumerate(OFFSETS):
            peer = peer_of(offset)
            copy = pltpu.make_async_remote_copy(
                src_ref=ins[a].at[:, block(peer, COLS)],
                dst_ref=outs[a].at[block(me, BLK), :],
                send_sem=send_sem.at[a, i],
                recv_sem=recv_sem.at[a, i],
                device_id={"seq": peer},
                device_id_type=MESH,
            )
            copy.start()
            copies.append(copy)
    for a in range(4):
        own = pltpu.make_async_copy(
            ins[a].at[:, block(me, COLS)], outs[a].at[block(me, BLK), :], own_sem.at[a]
        )
        own.start()
        copies.append(own)
    for copy in copies:
        copy.wait()


def heads_exchange(arrays):
    tokens = SEQ * BLK
    return pl.pallas_call(
        to_heads,
        out_shape=[jax.ShapeDtypeStruct((tokens, COLS), jnp.bfloat16)] * 4,
        in_specs=[pl.BlockSpec(memory_space=pltpu.HBM)] * 4,
        out_specs=[pl.BlockSpec(memory_space=pltpu.VMEM)] * 4,
        scratch_shapes=[
            pltpu.SemaphoreType.DMA((4, SEQ - 1)),
            pltpu.SemaphoreType.DMA((4, SEQ - 1)),
            pltpu.SemaphoreType.DMA((4,)),
        ],
        compiler_params=pltpu.CompilerParams(
            collective_id=0, has_side_effects=True, vmem_limit_bytes=58_500_000
        ),
    )(*arrays)


UNITS = 8
EARLY = 4
PIECE = 256
TURNS = (2, 2, 1, 1, 3, 3, 0, 0)
WIDE = 3 * COLS


def turn(at, by):
    return lax.rem(at + by, SIDE)


def finish(norm_factor, x_ref, early_ref, dq_ref, dk_ref, dv_ref, qg_ref, kg_ref, vg_ref, w_ref,
           xg, gt, prod, sib_in, y_out, y_in,
           load_sem, ring_send, ring_recv, back_send, back_recv, own_sem, sib_sem, y_sem):
    me, dp = lax.axis_index("seq"), lax.axis_index("dp")
    x, z, y, core = me // SIDE, lax.rem(me, SIDE), dp // 2, lax.rem(dp, 2)
    f32 = jnp.float32
    grads, homes = (dq_ref, dk_ref, dv_ref), (qg_ref, kg_ref, vg_ref)

    loads = {}
    for u in [*range(EARLY, UNITS), *range(EARLY)]:
        for part in (0, 1):
            spot = part * 2 + u % 2
            cols = slice(part * PIECE, (part + 1) * PIECE)
            if u < EARLY:
                at = (u // 2 * 4 + spot) * PIECE
                source, place = early_ref.at[:, :, :, at : at + PIECE], xg.at[u, :, :, :, cols]
            else:
                source = x_ref.at[:, block(turn(y, TURNS[u]) * 4 + spot, PIECE)]
                place = xg.at[u, x, z, :, cols]
            loads[u, part] = pltpu.make_async_copy(source, place, load_sem.at[u, part])
            loads[u, part].start()
    barrier = pltpu.get_barrier_semaphore()
    friends = [(peer_of(offset), dp) for offset in OFFSETS]
    friends += [(me, y * 2 + 1 - core)]
    friends += [(me, turn(y, by) * 2 + core) for by in (1, 2, 3)]
    for friend in friends:
        pl.semaphore_signal(barrier, inc=1, device_id=friend, device_id_type=MESH)
    pl.semaphore_wait(barrier, len(friends))

    started = []

    def send(src, dst, sems, device):
        copy = pltpu.make_async_remote_copy(
            src_ref=src, dst_ref=dst, send_sem=sems[0], recv_sem=sems[1],
            device_id=device, device_id_type=MESH,
        )
        copy.start()
        started.append(copy)
        return copy

    def ring(u, part, stage):
        cols = slice(part * PIECE, (part + 1) * PIECE)
        along_x = (part == 0) == (stage < 2)
        copies = []
        for way, step in enumerate((1, 3)):
            owner = 0 if stage % 2 == 0 else SIDE - step
            rows = slice(0, BLK) if stage % 2 == 0 else slice(way * (BLK // 2), (way + 1) * (BLK // 2))
            if along_x:
                device = (turn(x, step) * SIDE + z, dp)
                group = (turn(x, owner), z if stage < 2 else slice(None))
            else:
                device = (x * SIDE + turn(z, step), dp)
                group = (x if stage < 2 else slice(None), turn(z, owner))
            place = xg.at[u, group[0], group[1], rows, cols]
            at = (((u - EARLY) * 2 + part) * 4 + stage) * 2 + way
            copies.append(send(place, place, (ring_send.at[at], ring_recv.at[at]), device))
        return copies

    flights = {}

    def advance(u, stage):
        for part in (0, 1):
            if stage == 0:
                loads[u, part].wait()
            else:
                for copy in flights[u, part, stage - 1]:
                    copy.wait_recv()
            if stage < 4:
                flights[u, part, stage] = ring(u, part, stage)

    homeward, owns, siblings, across = [], [], {}, {}

    def go_home(a):
        for i, offset in enumerate(OFFSETS):
            peer = peer_of(offset)
            homeward.append(send(
                grads[a].at[block(peer, BLK), :], homes[a].at[:, block(me, COLS)],
                (back_send.at[a, i], back_recv.at[a, i]), (peer, dp),
            ))
        own = pltpu.make_async_copy(
            grads[a].at[block(me, BLK), :], homes[a].at[:, block(me, COLS)], own_sem.at[a]
        )
        own.start()
        owns.append(own)

    def product(u):
        @pl.loop(0, 2)
        def _(half):
            cols = block(lax.rem(1 - core + half, 2), PIECE)
            right = xg[u, :, :, :, cols].reshape(SEQ * BLK, PIECE)
            prod[u, half] = jnp.dot(gt[...], right, preferred_element_type=f32).astype(jnp.bfloat16)

        siblings[u] = send(
            prod.at[u, 0], sib_in.at[u], (sib_sem.at[0, u], sib_sem.at[1, u]),
            (me, y * 2 + 1 - core),
        )

    def settle(u):
        siblings[u].wait_recv()
        total = prod[u, 1].astype(f32) + sib_in[u].astype(f32)
        if u < UNITS - 2:
            y_out[u] = total.astype(jnp.bfloat16)
            across[u] = send(
                y_out.at[u], y_in.at[u], (y_sem.at[0, u], y_sem.at[1, u]),
                (me, turn(y, TURNS[u]) * 2 + core),
            )
        else:
            for i in range(u % 2, UNITS - 2, 2):
                across[i].wait_recv()
                total += y_in[i].astype(f32)
            for a in range(3):
                for h in range(2):
                    rows = slice(a * COLS + h * HDIM, a * COLS + (h + 1) * HDIM)
                    w_ref[a, (u % 2) * PIECE : (u % 2 + 1) * PIECE, h * HDIM : (h + 1) * HDIM] = (
                        total[rows].T * norm_factor
                    )

    late = range(EARLY, UNITS)
    for u in late:
        advance(u, 0)
    go_home(0)
    for u in late:
        advance(u, 1)
    for u in late:
        advance(u, 2)

    @pl.loop(0, SEQ)
    def _(n):
        for a in range(3):
            for h in range(2):
                tile = grads[a][block(n, BLK), h * HDIM : (h + 1) * HDIM]
                gt[a * COLS + h * HDIM : a * COLS + (h + 1) * HDIM, block(n, BLK)] = tile.T

    for u in range(EARLY):
        for part in (0, 1):
            loads[u, part].wait()
        product(u)
        if u >= 1:
            settle(u - 1)
    advance(EARLY, 3)
    if EARLY:
        settle(EARLY - 1)
    go_home(1)
    for u in late:
        if u + 1 < UNITS:
            advance(u + 1, 3)
        if u == UNITS - 2:
            go_home(2)
        advance(u, 4)
        product(u)
        settle(u)
    for copy in homeward:
        copy.wait_recv()
    for own in owns:
        own.wait()
    for copy in started:
        copy.wait_send()


def closing(norm_factor, layer_rows, early, dq, dk, dv):
    tokens, width = SEQ * BLK, layer_rows.shape[1]
    vmem, hbm = pl.BlockSpec(memory_space=pltpu.VMEM), pl.BlockSpec(memory_space=pltpu.HBM)
    bf16, f32 = jnp.bfloat16, jnp.float32
    rings = (UNITS - EARLY) * 16
    return pl.pallas_call(
        functools.partial(finish, norm_factor),
        out_shape=[jax.ShapeDtypeStruct((BLK, width), bf16)] * 3
        + [jax.ShapeDtypeStruct((3, 2 * PIECE, COLS), f32)],
        in_specs=[hbm, hbm, vmem, vmem, vmem],
        out_specs=[vmem] * 4,
        scratch_shapes=[
            pltpu.VMEM((UNITS, SIDE, SIDE, BLK, 2 * PIECE), bf16),
            pltpu.VMEM((WIDE, tokens), bf16),
            pltpu.VMEM((UNITS, 2, WIDE, PIECE), bf16),
            pltpu.VMEM((UNITS, WIDE, PIECE), bf16),
            pltpu.VMEM((UNITS - 2, WIDE, PIECE), bf16),
            pltpu.VMEM((UNITS - 2, WIDE, PIECE), bf16),
            pltpu.SemaphoreType.DMA((UNITS, 2)),
            pltpu.SemaphoreType.DMA((rings,)),
            pltpu.SemaphoreType.DMA((rings,)),
            pltpu.SemaphoreType.DMA((3, SEQ - 1)),
            pltpu.SemaphoreType.DMA((3, SEQ - 1)),
            pltpu.SemaphoreType.DMA((3,)),
            pltpu.SemaphoreType.DMA((2, UNITS)),
            pltpu.SemaphoreType.DMA((2, UNITS - 2)),
        ],
        compiler_params=pltpu.CompilerParams(
            collective_id=1, has_side_effects=True, vmem_limit_bytes=40 << 20
        ),
    )(layer_rows, early, dq, dk, dv)


def attend(kv_links, tallies, q_ref, k_ref, v_ref, g_ref, dq_ref, dk_ref, dv_ref, wq, turned, acc, sp):
    scale = HDIM ** (-0.5)
    heads = COLS // HDIM
    f32 = jnp.float32
    acc[...] = jnp.zeros_like(acc)
    wq[...] = jnp.zeros_like(wq)

    @pl.loop(0, NQB)
    def _(n):
        rows = pl.ds(pl.multiple_of(n * BLK, BLK), BLK)
        for h in range(heads):
            turned[h, n] = k_ref[rows, h * HDIM : (h + 1) * HDIM].astype(f32).T.astype(jnp.bfloat16)

    @pl.loop(0, NQB)
    def _(b):
        mine = pl.ds(pl.multiple_of(b * BLK, BLK), BLK)
        tally = tallies[b]

        def variant(slots):
            spans = [slice(h * HDIM, (h + 1) * HDIM) for h in range(heads)]
            rows = [block(kv_links[b, j], BLK) for j in range(slots)]
            for h in range(heads):
                wq[h, :HDIM, :HDIM] = q_ref[mine, spans[h]]
                wq[h, HDIM:, HDIM:] = g_ref[mine, spans[h]]
            tops = [None] * heads
            for j in range(slots):
                for h in range(heads):
                    kv = jnp.concatenate([k_ref[rows[j], spans[h]], v_ref[rows[j], spans[h]]], axis=1)
                    pair = lax.dot_general(
                        kv, wq[h], (((1,), (1,)), ((), ())), preferred_element_type=f32
                    )
                    score = pair[:, :HDIM]
                    if j == slots - 1 and slots > 1:
                        score = jnp.where(j < tally, score, -jnp.inf)
                    sp[h, j, :, :HDIM] = score
                    sp[h, j, :, HDIM:] = pair[:, HDIM:]
                    here = jnp.max(score.reshape(BLK // 8, 8, BLK), axis=0)
                    tops[h] = here if j == 0 else jnp.maximum(tops[h], here)
            tops = [jnp.max(top, axis=0, keepdims=True) for top in tops]
            totals, dots = [0.0] * heads, [0.0] * heads
            for j in range(slots):
                for h in range(heads):
                    weight = jnp.exp2((sp[h, j, :, :HDIM] - tops[h]) * (scale * LOG2E))
                    sp[h, j, :, :HDIM] = weight
                    totals[h] += jnp.sum(weight.reshape(BLK // 8, 8, BLK), axis=0)
                    slopes = weight * sp[h, j, :, HDIM:]
                    dots[h] += jnp.sum(slopes.reshape(BLK // 8, 8, BLK), axis=0)
            inverses = [1.0 / jnp.sum(total, axis=0, keepdims=True) for total in totals]
            dots = [jnp.sum(dot, axis=0, keepdims=True) * inv for dot, inv in zip(dots, inverses)]
            dqs = [0.0] * heads
            for j in range(slots):
                for h in range(heads):
                    prob = sp[h, j, :, :HDIM] * inverses[h]
                    slope = (prob * (sp[h, j, :, HDIM:] - dots[h])).astype(jnp.bfloat16)
                    left = jnp.concatenate([slope, prob.astype(jnp.bfloat16)], axis=1)
                    acc[h, rows[j], :] += jnp.dot(left, wq[h], preferred_element_type=f32)
                    dqs[h] += jnp.dot(turned[h, kv_links[b, j]], slope, preferred_element_type=f32)
            for h in range(heads):
                dq_ref[mine, spans[h]] = (dqs[h].T * scale).astype(jnp.bfloat16)

        for slots in range(2, MAXNB + 1, 2):
            pl.when((tally == slots) | (tally == slots - 1))(functools.partial(variant, slots))

    @pl.loop(0, NQB)
    def _(n):
        rows = pl.ds(pl.multiple_of(n * BLK, BLK), BLK)
        for h in range(heads):
            cols = slice(h * HDIM, (h + 1) * HDIM)
            dk_ref[rows, cols] = (acc[h, rows, :HDIM] * scale).astype(jnp.bfloat16)
            dv_ref[rows, cols] = acc[h, rows, HDIM:].astype(jnp.bfloat16)


def attention(links, tallies, q, k, v, g):
    tokens = NQB * BLK
    heads = COLS // HDIM
    spec = pl.BlockSpec(memory_space=pltpu.VMEM)
    smem = pl.BlockSpec(memory_space=pltpu.SMEM)
    flops = heads * NQB * MAXNB * 5 * 2 * BLK**3
    return pl.pallas_call(
        attend,
        out_shape=[jax.ShapeDtypeStruct((tokens, COLS), jnp.bfloat16)] * 3,
        in_specs=[smem, smem] + [spec] * 4,
        out_specs=[spec] * 3,
        scratch_shapes=[
            pltpu.VMEM((heads, 2 * HDIM, 2 * BLK), jnp.bfloat16),
            pltpu.VMEM((heads, NQB, HDIM, BLK), jnp.bfloat16),
            pltpu.VMEM((heads, tokens, 2 * HDIM), jnp.float32),
            pltpu.VMEM((heads, MAXNB, BLK, 2 * BLK), jnp.float32),
        ],
        compiler_params=pltpu.CompilerParams(vmem_limit_bytes=16 << 20),
        cost_estimate=pl.CostEstimate(
            flops=flops, bytes_accessed=7 * tokens * COLS * 2, transcendentals=heads * NQB * MAXNB * BLK * BLK
        ),
    )(links, tallies, q, k, v, g)


def gather_early(layer_rows):
    y = lax.axis_index("dp") // 2
    width = 4 * PIECE
    parts = [
        lax.dynamic_slice_in_dim(layer_rows, turn(y, TURNS[u]) * width, width, 1)
        for u in range(0, EARLY, 2)
    ]
    mine = jnp.concatenate(parts, axis=1)
    whole = lax.all_gather(mine[None], "seq", axis=1, tiled=True)
    return whole.reshape(SIDE, SIDE, BLK, EARLY // 2 * width)


def local(layer_input, query_rows, key_rows, value_rows, out_grad, neighbours, counts):
    early = gather_early(layer_input[0])
    q, k, v, g = heads_exchange([query_rows[0], key_rows[0], value_rows[0], out_grad[0]])
    dq, dk, dv = attention(neighbours[0], counts[0], q, k, v, g)
    norm_factor = 1.0 / math.sqrt(SEQ * BLK * lax.axis_size("dp"))
    query_grad, key_grad, value_grad, owned = closing(norm_factor, layer_input[0], early, dq, dk, dv)
    return query_grad[None], key_grad[None], value_grad[None], owned


def solution(mesh):
    rows = P("dp", "seq", None)
    return jax.shard_map(
        local,
        mesh=mesh,
        in_specs=(rows,) * 5 + (P("dp", None, None), P("dp", None)),
        out_specs=(rows, rows, rows, P(None, "dp", "seq")),
        check_vma=False,
    )
```

```python
import functools
import math

import jax
import jax.numpy as jnp
from jax import lax
from jax.experimental import pallas as pl
from jax.experimental.pallas import tpu as pltpu
from jax.sharding import PartitionSpec as P

HDIM = 128
BLK = 128
MAXNB = 8
NQB = 16
SEQ = 16
SIDE = 4
COLS = 256
LOG2E = 1.4426950408889634
MESH = pl.DeviceIdType.MESH


OFFSETS = (
    (2, 2), (2, 1), (2, 3), (1, 2), (3, 2), (2, 0), (0, 2), (1, 1),
    (3, 3), (1, 3), (3, 1), (1, 0), (3, 0), (0, 1), (0, 3),
)


def peer_of(offset):
    me, core = lax.axis_index("seq"), lax.rem(lax.axis_index("dp"), 2)
    place = []
    for at, step in zip((me // SIDE, lax.rem(me, SIDE)), offset):
        back = (SIDE - step) % SIDE
        place.append(lax.rem(at + step + core * (back - step), SIDE))
    return place[0] * SIDE + place[1]


def block(index, size):
    return pl.ds(pl.multiple_of(index * size, size), size)


def to_heads(*refs):
    ins, outs = refs[:4], refs[4:8]
    send_sem, recv_sem, own_sem = refs[8:]
    me = lax.axis_index("seq")
    barrier = pltpu.get_barrier_semaphore()
    for offset in OFFSETS:
        pl.semaphore_signal(
            barrier, inc=1, device_id={"seq": peer_of(offset)}, device_id_type=MESH
        )
    pl.semaphore_wait(barrier, SEQ - 1)
    copies = []
    for a in range(4):
        for i, offset in enumerate(OFFSETS):
            peer = peer_of(offset)
            copy = pltpu.make_async_remote_copy(
                src_ref=ins[a].at[:, block(peer, COLS)],
                dst_ref=outs[a].at[block(me, BLK), :],
                send_sem=send_sem.at[a, i],
                recv_sem=recv_sem.at[a, i],
                device_id={"seq": peer},
                device_id_type=MESH,
            )
            copy.start()
            copies.append(copy)
    for a in range(4):
        own = pltpu.make_async_copy(
            ins[a].at[:, block(me, COLS)], outs[a].at[block(me, BLK), :], own_sem.at[a]
        )
        own.start()
        copies.append(own)
    for copy in copies:
        copy.wait()


def heads_exchange(arrays):
    tokens = SEQ * BLK
    return pl.pallas_call(
        to_heads,
        out_shape=[jax.ShapeDtypeStruct((tokens, COLS), jnp.bfloat16)] * 4,
        in_specs=[pl.BlockSpec(memory_space=pltpu.HBM)] * 4,
        out_specs=[pl.BlockSpec(memory_space=pltpu.VMEM)] * 4,
        scratch_shapes=[
            pltpu.SemaphoreType.DMA((4, SEQ - 1)),
            pltpu.SemaphoreType.DMA((4, SEQ - 1)),
            pltpu.SemaphoreType.DMA((4,)),
        ],
        compiler_params=pltpu.CompilerParams(
            collective_id=0, has_side_effects=True, vmem_limit_bytes=58_500_000
        ),
    )(*arrays)


UNITS = 8
EARLY = 4
PIECE = 256
TURNS = (2, 2, 1, 1, 3, 3, 0, 0)
WIDE = 3 * COLS


def turn(at, by):
    return lax.rem(at + by, SIDE)


def finish(norm_factor, x_ref, early_ref, dq_ref, dk_ref, dv_ref, qg_ref, kg_ref, vg_ref, w_ref,
           xg, gt, prod, sib_in, y_out, y_in,
           load_sem, ring_send, ring_recv, back_send, back_recv, own_sem, sib_sem, y_sem):
    me, dp = lax.axis_index("seq"), lax.axis_index("dp")
    x, z, y, core = me // SIDE, lax.rem(me, SIDE), dp // 2, lax.rem(dp, 2)
    f32 = jnp.float32
    grads, homes = (dq_ref, dk_ref, dv_ref), (qg_ref, kg_ref, vg_ref)

    loads = {}
    for u in [*range(EARLY, UNITS), *range(EARLY)]:
        for part in (0, 1):
            spot = part * 2 + u % 2
            cols = slice(part * PIECE, (part + 1) * PIECE)
            if u < EARLY:
                at = (u // 2 * 4 + spot) * PIECE
                source, place = early_ref.at[:, :, :, at : at + PIECE], xg.at[u, :, :, :, cols]
            else:
                source = x_ref.at[:, block(turn(y, TURNS[u]) * 4 + spot, PIECE)]
                place = xg.at[u, x, z, :, cols]
            loads[u, part] = pltpu.make_async_copy(source, place, load_sem.at[u, part])
            loads[u, part].start()
    barrier = pltpu.get_barrier_semaphore()
    friends = [(peer_of(offset), dp) for offset in OFFSETS]
    friends += [(me, y * 2 + 1 - core)]
    friends += [(me, turn(y, by) * 2 + core) for by in (1, 2, 3)]
    for friend in friends:
        pl.semaphore_signal(barrier, inc=1, device_id=friend, device_id_type=MESH)
    pl.semaphore_wait(barrier, len(friends))

    started = []

    def send(src, dst, sems, device):
        copy = pltpu.make_async_remote_copy(
            src_ref=src, dst_ref=dst, send_sem=sems[0], recv_sem=sems[1],
            device_id=device, device_id_type=MESH,
        )
        copy.start()
        started.append(copy)
        return copy

    def ring(u, part, stage):
        cols = slice(part * PIECE, (part + 1) * PIECE)
        along_x = (part == 0) == (stage < 2)
        copies = []
        for way, step in enumerate((1, 3)):
            owner = 0 if stage % 2 == 0 else SIDE - step
            rows = slice(0, BLK) if stage % 2 == 0 else slice(way * (BLK // 2), (way + 1) * (BLK // 2))
            if along_x:
                device = (turn(x, step) * SIDE + z, dp)
                group = (turn(x, owner), z if stage < 2 else slice(None))
            else:
                device = (x * SIDE + turn(z, step), dp)
                group = (x if stage < 2 else slice(None), turn(z, owner))
            place = xg.at[u, group[0], group[1], rows, cols]
            at = (((u - EARLY) * 2 + part) * 4 + stage) * 2 + way
            copies.append(send(place, place, (ring_send.at[at], ring_recv.at[at]), device))
        return copies

    flights = {}

    def advance(u, stage):
        for part in (0, 1):
            if stage == 0:
                loads[u, part].wait()
            else:
                for copy in flights[u, part, stage - 1]:
                    copy.wait_recv()
            if stage < 4:
                flights[u, part, stage] = ring(u, part, stage)

    homeward, owns, siblings, across = [], [], {}, {}

    def go_home(a):
        for i, offset in enumerate(OFFSETS):
            peer = peer_of(offset)
            homeward.append(send(
                grads[a].at[block(peer, BLK), :], homes[a].at[:, block(me, COLS)],
                (back_send.at[a, i], back_recv.at[a, i]), (peer, dp),
            ))
        own = pltpu.make_async_copy(
            grads[a].at[block(me, BLK), :], homes[a].at[:, block(me, COLS)], own_sem.at[a]
        )
        own.start()
        owns.append(own)

    def product(u):
        @pl.loop(0, 2)
        def _(half):
            cols = block(lax.rem(1 - core + half, 2), PIECE)
            right = xg[u, :, :, :, cols].reshape(SEQ * BLK, PIECE)
            prod[u, half] = jnp.dot(gt[...], right, preferred_element_type=f32).astype(jnp.bfloat16)

        siblings[u] = send(
            prod.at[u, 0], sib_in.at[u], (sib_sem.at[0, u], sib_sem.at[1, u]),
            (me, y * 2 + 1 - core),
        )

    def settle(u):
        siblings[u].wait_recv()
        total = prod[u, 1].astype(f32) + sib_in[u].astype(f32)
        if u < UNITS - 2:
            y_out[u] = total.astype(jnp.bfloat16)
            across[u] = send(
                y_out.at[u], y_in.at[u], (y_sem.at[0, u], y_sem.at[1, u]),
                (me, turn(y, TURNS[u]) * 2 + core),
            )
        else:
            for i in range(u % 2, UNITS - 2, 2):
                across[i].wait_recv()
                total += y_in[i].astype(f32)
            for a in range(3):
                for h in range(2):
                    rows = slice(a * COLS + h * HDIM, a * COLS + (h + 1) * HDIM)
                    w_ref[a, (u % 2) * PIECE : (u % 2 + 1) * PIECE, h * HDIM : (h + 1) * HDIM] = (
                        total[rows].T * norm_factor
                    )

    late = range(EARLY, UNITS)
    for u in late:
        advance(u, 0)
    go_home(0)
    for u in late:
        advance(u, 1)
    for u in late:
        advance(u, 2)

    @pl.loop(0, SEQ)
    def _(n):
        for a in range(3):
            for h in range(2):
                tile = grads[a][block(n, BLK), h * HDIM : (h + 1) * HDIM]
                gt[a * COLS + h * HDIM : a * COLS + (h + 1) * HDIM, block(n, BLK)] = tile.T

    ahead, leaving = EARLY, True
    for u in range(EARLY):
        for part in (0, 1):
            loads[u, part].wait()
        product(u)
        advance(ahead, 3)
        ahead += 1
        if u:
            settle(u - 1)
        if u == min(2, EARLY - 1):
            go_home(1)
    settle(EARLY - 1)
    for u in late:
        if ahead < UNITS:
            advance(ahead, 3)
            ahead += 1
        advance(u, 4)
        product(u)
        settle(u)
        if leaving and ahead == UNITS:
            go_home(2)
            leaving = False
    for copy in homeward:
        copy.wait_recv()
    for own in owns:
        own.wait()
    for copy in started:
        copy.wait_send()


def closing(norm_factor, layer_rows, early, dq, dk, dv):
    tokens, width = SEQ * BLK, layer_rows.shape[1]
    vmem, hbm = pl.BlockSpec(memory_space=pltpu.VMEM), pl.BlockSpec(memory_space=pltpu.HBM)
    bf16, f32 = jnp.bfloat16, jnp.float32
    rings = (UNITS - EARLY) * 16
    return pl.pallas_call(
        functools.partial(finish, norm_factor),
        out_shape=[jax.ShapeDtypeStruct((BLK, width), bf16)] * 3
        + [jax.ShapeDtypeStruct((3, 2 * PIECE, COLS), f32)],
        in_specs=[hbm, hbm, vmem, vmem, vmem],
        out_specs=[vmem] * 4,
        scratch_shapes=[
            pltpu.VMEM((UNITS, SIDE, SIDE, BLK, 2 * PIECE), bf16),
            pltpu.VMEM((WIDE, tokens), bf16),
            pltpu.VMEM((UNITS, 2, WIDE, PIECE), bf16),
            pltpu.VMEM((UNITS, WIDE, PIECE), bf16),
            pltpu.VMEM((UNITS - 2, WIDE, PIECE), bf16),
            pltpu.VMEM((UNITS - 2, WIDE, PIECE), bf16),
            pltpu.SemaphoreType.DMA((UNITS, 2)),
            pltpu.SemaphoreType.DMA((rings,)),
            pltpu.SemaphoreType.DMA((rings,)),
            pltpu.SemaphoreType.DMA((3, SEQ - 1)),
            pltpu.SemaphoreType.DMA((3, SEQ - 1)),
            pltpu.SemaphoreType.DMA((3,)),
            pltpu.SemaphoreType.DMA((2, UNITS)),
            pltpu.SemaphoreType.DMA((2, UNITS - 2)),
        ],
        compiler_params=pltpu.CompilerParams(
            collective_id=1, has_side_effects=True, vmem_limit_bytes=40 << 20
        ),
    )(layer_rows, early, dq, dk, dv)


def attend(kv_links, tallies, q_ref, k_ref, v_ref, g_ref, dq_ref, dk_ref, dv_ref, wq, turned, acc, sp):
    scale = HDIM ** (-0.5)
    heads = COLS // HDIM
    f32 = jnp.float32
    acc[...] = jnp.zeros_like(acc)
    wq[...] = jnp.zeros_like(wq)

    @pl.loop(0, NQB)
    def _(n):
        rows = pl.ds(pl.multiple_of(n * BLK, BLK), BLK)
        for h in range(heads):
            turned[h, n] = k_ref[rows, h * HDIM : (h + 1) * HDIM].astype(f32).T.astype(jnp.bfloat16)

    @pl.loop(0, NQB)
    def _(b):
        mine = pl.ds(pl.multiple_of(b * BLK, BLK), BLK)
        tally = tallies[b]

        def variant(slots):
            spans = [slice(h * HDIM, (h + 1) * HDIM) for h in range(heads)]
            rows = [block(kv_links[b, j], BLK) for j in range(slots)]
            for h in range(heads):
                wq[h, :HDIM, :HDIM] = q_ref[mine, spans[h]]
                wq[h, HDIM:, HDIM:] = g_ref[mine, spans[h]]
            tops = [None] * heads
            for j in range(slots):
                for h in range(heads):
                    kv = jnp.concatenate([k_ref[rows[j], spans[h]], v_ref[rows[j], spans[h]]], axis=1)
                    pair = lax.dot_general(
                        kv, wq[h], (((1,), (1,)), ((), ())), preferred_element_type=f32
                    )
                    score = pair[:, :HDIM]
                    if j == slots - 1 and slots > 1:
                        score = jnp.where(j < tally, score, -jnp.inf)
                    sp[h, j, :, :HDIM] = score
                    sp[h, j, :, HDIM:] = pair[:, HDIM:]
                    here = jnp.max(score.reshape(BLK // 8, 8, BLK), axis=0)
                    tops[h] = here if j == 0 else jnp.maximum(tops[h], here)
            tops = [jnp.max(top, axis=0, keepdims=True) for top in tops]
            totals, dots = [0.0] * heads, [0.0] * heads
            for j in range(slots):
                for h in range(heads):
                    weight = jnp.exp2((sp[h, j, :, :HDIM] - tops[h]) * (scale * LOG2E))
                    sp[h, j, :, :HDIM] = weight
                    totals[h] += jnp.sum(weight.reshape(BLK // 8, 8, BLK), axis=0)
                    slopes = weight * sp[h, j, :, HDIM:]
                    dots[h] += jnp.sum(slopes.reshape(BLK // 8, 8, BLK), axis=0)
            inverses = [1.0 / jnp.sum(total, axis=0, keepdims=True) for total in totals]
            dots = [jnp.sum(dot, axis=0, keepdims=True) * inv for dot, inv in zip(dots, inverses)]
            dqs = [0.0] * heads
            for j in range(slots):
                for h in range(heads):
                    prob = sp[h, j, :, :HDIM] * inverses[h]
                    slope = (prob * (sp[h, j, :, HDIM:] - dots[h])).astype(jnp.bfloat16)
                    left = jnp.concatenate([slope, prob.astype(jnp.bfloat16)], axis=1)
                    acc[h, rows[j], :] += jnp.dot(left, wq[h], preferred_element_type=f32)
                    dqs[h] += jnp.dot(turned[h, kv_links[b, j]], slope, preferred_element_type=f32)
            for h in range(heads):
                dq_ref[mine, spans[h]] = (dqs[h].T * scale).astype(jnp.bfloat16)

        for slots in range(2, MAXNB + 1, 2):
            pl.when((tally == slots) | (tally == slots - 1))(functools.partial(variant, slots))

    @pl.loop(0, NQB)
    def _(n):
        rows = pl.ds(pl.multiple_of(n * BLK, BLK), BLK)
        for h in range(heads):
            cols = slice(h * HDIM, (h + 1) * HDIM)
            dk_ref[rows, cols] = (acc[h, rows, :HDIM] * scale).astype(jnp.bfloat16)
            dv_ref[rows, cols] = acc[h, rows, HDIM:].astype(jnp.bfloat16)


def attention(links, tallies, q, k, v, g):
    tokens = NQB * BLK
    heads = COLS // HDIM
    spec = pl.BlockSpec(memory_space=pltpu.VMEM)
    smem = pl.BlockSpec(memory_space=pltpu.SMEM)
    flops = heads * NQB * MAXNB * 5 * 2 * BLK**3
    return pl.pallas_call(
        attend,
        out_shape=[jax.ShapeDtypeStruct((tokens, COLS), jnp.bfloat16)] * 3,
        in_specs=[smem, smem] + [spec] * 4,
        out_specs=[spec] * 3,
        scratch_shapes=[
            pltpu.VMEM((heads, 2 * HDIM, 2 * BLK), jnp.bfloat16),
            pltpu.VMEM((heads, NQB, HDIM, BLK), jnp.bfloat16),
            pltpu.VMEM((heads, tokens, 2 * HDIM), jnp.float32),
            pltpu.VMEM((heads, MAXNB, BLK, 2 * BLK), jnp.float32),
        ],
        compiler_params=pltpu.CompilerParams(vmem_limit_bytes=16 << 20),
        cost_estimate=pl.CostEstimate(
            flops=flops, bytes_accessed=7 * tokens * COLS * 2, transcendentals=heads * NQB * MAXNB * BLK * BLK
        ),
    )(links, tallies, q, k, v, g)


def gather_early(layer_rows):
    y = lax.axis_index("dp") // 2
    width = 4 * PIECE
    parts = [
        lax.dynamic_slice_in_dim(layer_rows, turn(y, TURNS[u]) * width, width, 1)
        for u in range(0, EARLY, 2)
    ]
    mine = jnp.concatenate(parts, axis=1)
    whole = lax.all_gather(mine[None], "seq", axis=1, tiled=True)
    return whole.reshape(SIDE, SIDE, BLK, EARLY // 2 * width)


def hand_over(*refs):
    ins, outs, sem = refs[:4], refs[4:8], refs[8]
    copies = [pltpu.make_async_copy(a, b, sem.at[i]) for i, (a, b) in enumerate(zip(ins, outs))]
    for copy in copies:
        copy.start()
    for copy in copies:
        copy.wait()


def settled(arrays):
    return pl.pallas_call(
        hand_over,
        out_shape=[jax.ShapeDtypeStruct(a.shape, a.dtype) for a in arrays],
        in_specs=[pl.BlockSpec(memory_space=pltpu.VMEM)] * 4,
        out_specs=[pl.BlockSpec(memory_space=pltpu.HBM)] * 4,
        scratch_shapes=[pltpu.SemaphoreType.DMA((4,))],
        compiler_params=pltpu.CompilerParams(vmem_limit_bytes=8 << 20),
    )(*arrays)


def local(layer_input, query_rows, key_rows, value_rows, out_grad, neighbours, counts):
    early = gather_early(layer_input[0])
    q, k, v, g = heads_exchange([query_rows[0], key_rows[0], value_rows[0], out_grad[0]])
    dq, dk, dv = attention(neighbours[0], counts[0], q, k, v, g)
    norm_factor = 1.0 / math.sqrt(SEQ * BLK * lax.axis_size("dp"))
    query_grad, key_grad, value_grad, owned = settled(
        closing(norm_factor, layer_input[0], early, dq, dk, dv)
    )
    return query_grad[None], key_grad[None], value_grad[None], owned


def solution(mesh):
    rows = P("dp", "seq", None)
    return jax.shard_map(
        local,
        mesh=mesh,
        in_specs=(rows,) * 5 + (P("dp", None, None), P("dp", None)),
        out_specs=(rows, rows, rows, P(None, "dp", "seq")),
        check_vma=False,
    )
```

```python
import functools
import math

import jax
import jax.numpy as jnp
from jax import lax
from jax.experimental import pallas as pl
from jax.experimental.pallas import tpu as pltpu
from jax.sharding import PartitionSpec as P

HDIM = 128
BLK = 128
MAXNB = 8
NQB = 16
SEQ = 16
SIDE = 4
COLS = 256
LOG2E = 1.4426950408889634
MESH = pl.DeviceIdType.MESH


OFFSETS = (
    (2, 2), (2, 1), (2, 3), (1, 2), (3, 2), (2, 0), (0, 2), (1, 1),
    (3, 3), (1, 3), (3, 1), (1, 0), (3, 0), (0, 1), (0, 3),
)


def peer_of(offset):
    me, core = lax.axis_index("seq"), lax.rem(lax.axis_index("dp"), 2)
    place = []
    for at, step in zip((me // SIDE, lax.rem(me, SIDE)), offset):
        back = (SIDE - step) % SIDE
        place.append(lax.rem(at + step + core * (back - step), SIDE))
    return place[0] * SIDE + place[1]


WINDOW = 1


def block(index, size):
    return pl.ds(pl.multiple_of(index * size, size), size)


def to_heads(*refs):
    ins, outs = refs[:4], refs[4:8]
    send_sem, recv_sem, own_sem = refs[8:]
    me = lax.axis_index("seq")
    barrier = pltpu.get_barrier_semaphore()
    for offset in OFFSETS:
        pl.semaphore_signal(
            barrier, inc=1, device_id={"seq": peer_of(offset)}, device_id_type=MESH
        )
    pl.semaphore_wait(barrier, SEQ - 1)
    groups = []
    for a in range(4):
        if a >= WINDOW:
            for copy in groups[a - WINDOW]:
                copy.wait_send()
        groups.append([])
        for i, offset in enumerate(OFFSETS):
            peer = peer_of(offset)
            copy = pltpu.make_async_remote_copy(
                src_ref=ins[a].at[:, block(peer, COLS)],
                dst_ref=outs[a].at[block(me, BLK), :],
                send_sem=send_sem.at[a, i],
                recv_sem=recv_sem.at[a, i],
                device_id={"seq": peer},
                device_id_type=MESH,
            )
            copy.start()
            groups[a].append(copy)
    owns = []
    for a in range(4):
        own = pltpu.make_async_copy(
            ins[a].at[:, block(me, COLS)], outs[a].at[block(me, BLK), :], own_sem.at[a]
        )
        own.start()
        owns.append(own)
    for group in groups[4 - WINDOW :]:
        for copy in group:
            copy.wait_send()
    for group in groups:
        for copy in group:
            copy.wait_recv()
    for own in owns:
        own.wait()


def heads_exchange(arrays):
    tokens = SEQ * BLK
    return pl.pallas_call(
        to_heads,
        out_shape=[jax.ShapeDtypeStruct((tokens, COLS), jnp.bfloat16)] * 4,
        in_specs=[pl.BlockSpec(memory_space=pltpu.HBM)] * 4,
        out_specs=[pl.BlockSpec(memory_space=pltpu.VMEM)] * 4,
        scratch_shapes=[
            pltpu.SemaphoreType.DMA((4, SEQ - 1)),
            pltpu.SemaphoreType.DMA((4, SEQ - 1)),
            pltpu.SemaphoreType.DMA((4,)),
        ],
        compiler_params=pltpu.CompilerParams(
            collective_id=0, has_side_effects=True, vmem_limit_bytes=58_500_000
        ),
    )(*arrays)


UNITS = 8
EARLY = 4
PIECE = 256
TURNS = (2, 2, 1, 1, 3, 3, 0, 0)
WIDE = 3 * COLS


def turn(at, by):
    return lax.rem(at + by, SIDE)


def finish(norm_factor, x_ref, early_ref, dq_ref, dk_ref, dv_ref, qg_ref, kg_ref, vg_ref, w_ref,
           xg, gt, prod, sib_in, y_out, y_in,
           load_sem, ring_send, ring_recv, back_send, back_recv, own_sem, sib_sem, y_sem):
    me, dp = lax.axis_index("seq"), lax.axis_index("dp")
    x, z, y, core = me // SIDE, lax.rem(me, SIDE), dp // 2, lax.rem(dp, 2)
    f32 = jnp.float32
    grads, homes = (dq_ref, dk_ref, dv_ref), (qg_ref, kg_ref, vg_ref)

    loads = {}
    for u in [*range(EARLY, UNITS), *range(EARLY)]:
        for part in (0, 1):
            spot = part * 2 + u % 2
            cols = slice(part * PIECE, (part + 1) * PIECE)
            if u < EARLY:
                at = (u // 2 * 4 + spot) * PIECE
                source, place = early_ref.at[:, :, :, at : at + PIECE], xg.at[u, :, :, :, cols]
            else:
                source = x_ref.at[:, block(turn(y, TURNS[u]) * 4 + spot, PIECE)]
                place = xg.at[u, x, z, :, cols]
            loads[u, part] = pltpu.make_async_copy(source, place, load_sem.at[u, part])
            loads[u, part].start()
    barrier = pltpu.get_barrier_semaphore()
    friends = [(peer_of(offset), dp) for offset in OFFSETS]
    friends += [(me, y * 2 + 1 - core)]
    friends += [(me, turn(y, by) * 2 + core) for by in (1, 2, 3)]
    for friend in friends:
        pl.semaphore_signal(barrier, inc=1, device_id=friend, device_id_type=MESH)
    pl.semaphore_wait(barrier, len(friends))

    started = []

    def send(src, dst, sems, device):
        copy = pltpu.make_async_remote_copy(
            src_ref=src, dst_ref=dst, send_sem=sems[0], recv_sem=sems[1],
            device_id=device, device_id_type=MESH,
        )
        copy.start()
        started.append(copy)
        return copy

    def ring(u, part, stage):
        cols = slice(part * PIECE, (part + 1) * PIECE)
        along_x = (part == 0) == (stage < 2)
        copies = []
        for way, step in enumerate((1, 3)):
            owner = 0 if stage % 2 == 0 else SIDE - step
            rows = slice(0, BLK) if stage % 2 == 0 else slice(way * (BLK // 2), (way + 1) * (BLK // 2))
            if along_x:
                device = (turn(x, step) * SIDE + z, dp)
                group = (turn(x, owner), z if stage < 2 else slice(None))
            else:
                device = (x * SIDE + turn(z, step), dp)
                group = (x if stage < 2 else slice(None), turn(z, owner))
            place = xg.at[u, group[0], group[1], rows, cols]
            at = (((u - EARLY) * 2 + part) * 4 + stage) * 2 + way
            copies.append(send(place, place, (ring_send.at[at], ring_recv.at[at]), device))
        return copies

    flights = {}

    def advance(u, stage):
        for part in (0, 1):
            if stage == 0:
                loads[u, part].wait()
            else:
                for copy in flights[u, part, stage - 1]:
                    copy.wait_recv()
            if stage < 4:
                flights[u, part, stage] = ring(u, part, stage)

    homeward, owns, siblings, across = [], [], {}, {}

    def go_home(a):
        for i, offset in enumerate(OFFSETS):
            peer = peer_of(offset)
            homeward.append(send(
                grads[a].at[block(peer, BLK), :], homes[a].at[:, block(me, COLS)],
                (back_send.at[a, i], back_recv.at[a, i]), (peer, dp),
            ))
        own = pltpu.make_async_copy(
            grads[a].at[block(me, BLK), :], homes[a].at[:, block(me, COLS)], own_sem.at[a]
        )
        own.start()
        owns.append(own)

    def product(u):
        @pl.loop(0, 2)
        def _(half):
            cols = block(lax.rem(1 - core + half, 2), PIECE)
            right = xg[u, :, :, :, cols].reshape(SEQ * BLK, PIECE)
            prod[u, half] = jnp.dot(gt[...], right, preferred_element_type=f32).astype(jnp.bfloat16)

        siblings[u] = send(
            prod.at[u, 0], sib_in.at[u], (sib_sem.at[0, u], sib_sem.at[1, u]),
            (me, y * 2 + 1 - core),
        )

    def settle(u):
        siblings[u].wait_recv()
        total = prod[u, 1].astype(f32) + sib_in[u].astype(f32)
        if u < UNITS - 2:
            y_out[u] = total.astype(jnp.bfloat16)
            across[u] = send(
                y_out.at[u], y_in.at[u], (y_sem.at[0, u], y_sem.at[1, u]),
                (me, turn(y, TURNS[u]) * 2 + core),
            )
        else:
            for i in range(u % 2, UNITS - 2, 2):
                across[i].wait_recv()
                total += y_in[i].astype(f32)
            for a in range(3):
                for h in range(2):
                    rows = slice(a * COLS + h * HDIM, a * COLS + (h + 1) * HDIM)
                    w_ref[a, (u % 2) * PIECE : (u % 2 + 1) * PIECE, h * HDIM : (h + 1) * HDIM] = (
                        total[rows].T * norm_factor
                    )

    late = range(EARLY, UNITS)
    for u in late:
        advance(u, 0)
    go_home(0)
    for u in late:
        advance(u, 1)
    for u in late:
        advance(u, 2)

    @pl.loop(0, SEQ)
    def _(n):
        for a in range(3):
            for h in range(2):
                tile = grads[a][block(n, BLK), h * HDIM : (h + 1) * HDIM]
                gt[a * COLS + h * HDIM : a * COLS + (h + 1) * HDIM, block(n, BLK)] = tile.T

    ahead, leaving = EARLY, True
    for u in range(EARLY):
        for part in (0, 1):
            loads[u, part].wait()
        product(u)
        advance(ahead, 3)
        ahead += 1
        if u:
            settle(u - 1)
        if u == min(2, EARLY - 1):
            go_home(1)
    settle(EARLY - 1)
    for u in late:
        if ahead < UNITS:
            advance(ahead, 3)
            ahead += 1
        advance(u, 4)
        product(u)
        settle(u)
        if leaving and ahead == UNITS:
            go_home(2)
            leaving = False
    for copy in homeward:
        copy.wait_recv()
    for own in owns:
        own.wait()
    for copy in started:
        copy.wait_send()


def closing(norm_factor, layer_rows, early, dq, dk, dv):
    tokens, width = SEQ * BLK, layer_rows.shape[1]
    vmem, hbm = pl.BlockSpec(memory_space=pltpu.VMEM), pl.BlockSpec(memory_space=pltpu.HBM)
    bf16, f32 = jnp.bfloat16, jnp.float32
    rings = (UNITS - EARLY) * 16
    return pl.pallas_call(
        functools.partial(finish, norm_factor),
        out_shape=[jax.ShapeDtypeStruct((BLK, width), bf16)] * 3
        + [jax.ShapeDtypeStruct((3, 2 * PIECE, COLS), f32)],
        in_specs=[hbm, hbm, vmem, vmem, vmem],
        out_specs=[vmem] * 4,
        scratch_shapes=[
            pltpu.VMEM((UNITS, SIDE, SIDE, BLK, 2 * PIECE), bf16),
            pltpu.VMEM((WIDE, tokens), bf16),
            pltpu.VMEM((UNITS, 2, WIDE, PIECE), bf16),
            pltpu.VMEM((UNITS, WIDE, PIECE), bf16),
            pltpu.VMEM((UNITS - 2, WIDE, PIECE), bf16),
            pltpu.VMEM((UNITS - 2, WIDE, PIECE), bf16),
            pltpu.SemaphoreType.DMA((UNITS, 2)),
            pltpu.SemaphoreType.DMA((rings,)),
            pltpu.SemaphoreType.DMA((rings,)),
            pltpu.SemaphoreType.DMA((3, SEQ - 1)),
            pltpu.SemaphoreType.DMA((3, SEQ - 1)),
            pltpu.SemaphoreType.DMA((3,)),
            pltpu.SemaphoreType.DMA((2, UNITS)),
            pltpu.SemaphoreType.DMA((2, UNITS - 2)),
        ],
        compiler_params=pltpu.CompilerParams(
            collective_id=1, has_side_effects=True, vmem_limit_bytes=40 << 20
        ),
    )(layer_rows, early, dq, dk, dv)


def attend(kv_links, tallies, q_ref, k_ref, v_ref, g_ref, dq_ref, dk_ref, dv_ref, wq, turned, acc, sp):
    scale = HDIM ** (-0.5)
    heads = COLS // HDIM
    f32 = jnp.float32
    acc[...] = jnp.zeros_like(acc)
    wq[...] = jnp.zeros_like(wq)

    @pl.loop(0, NQB)
    def _(n):
        rows = pl.ds(pl.multiple_of(n * BLK, BLK), BLK)
        for h in range(heads):
            turned[h, n] = k_ref[rows, h * HDIM : (h + 1) * HDIM].astype(f32).T.astype(jnp.bfloat16)

    @pl.loop(0, NQB)
    def _(b):
        mine = pl.ds(pl.multiple_of(b * BLK, BLK), BLK)
        tally = tallies[b]

        def variant(slots):
            spans = [slice(h * HDIM, (h + 1) * HDIM) for h in range(heads)]
            rows = [block(kv_links[b, j], BLK) for j in range(slots)]
            for h in range(heads):
                wq[h, :HDIM, :HDIM] = q_ref[mine, spans[h]]
                wq[h, HDIM:, HDIM:] = g_ref[mine, spans[h]]
            tops = [None] * heads
            for j in range(slots):
                for h in range(heads):
                    kv = jnp.concatenate([k_ref[rows[j], spans[h]], v_ref[rows[j], spans[h]]], axis=1)
                    pair = lax.dot_general(
                        kv, wq[h], (((1,), (1,)), ((), ())), preferred_element_type=f32
                    )
                    score = pair[:, :HDIM]
                    if j == slots - 1 and slots > 1:
                        score = jnp.where(j < tally, score, -jnp.inf)
                    sp[h, j, :, :HDIM] = score
                    sp[h, j, :, HDIM:] = pair[:, HDIM:]
                    here = jnp.max(score.reshape(BLK // 8, 8, BLK), axis=0)
                    tops[h] = here if j == 0 else jnp.maximum(tops[h], here)
            tops = [jnp.max(top, axis=0, keepdims=True) for top in tops]
            totals, dots = [0.0] * heads, [0.0] * heads
            for j in range(slots):
                for h in range(heads):
                    weight = jnp.exp2((sp[h, j, :, :HDIM] - tops[h]) * (scale * LOG2E))
                    sp[h, j, :, :HDIM] = weight
                    totals[h] += jnp.sum(weight.reshape(BLK // 8, 8, BLK), axis=0)
                    slopes = weight * sp[h, j, :, HDIM:]
                    dots[h] += jnp.sum(slopes.reshape(BLK // 8, 8, BLK), axis=0)
            inverses = [1.0 / jnp.sum(total, axis=0, keepdims=True) for total in totals]
            dots = [jnp.sum(dot, axis=0, keepdims=True) * inv for dot, inv in zip(dots, inverses)]
            dqs = [0.0] * heads
            for j in range(slots):
                for h in range(heads):
                    prob = sp[h, j, :, :HDIM] * inverses[h]
                    slope = (prob * (sp[h, j, :, HDIM:] - dots[h])).astype(jnp.bfloat16)
                    left = jnp.concatenate([slope, prob.astype(jnp.bfloat16)], axis=1)
                    acc[h, rows[j], :] += jnp.dot(left, wq[h], preferred_element_type=f32)
                    dqs[h] += jnp.dot(turned[h, kv_links[b, j]], slope, preferred_element_type=f32)
            for h in range(heads):
                dq_ref[mine, spans[h]] = (dqs[h].T * scale).astype(jnp.bfloat16)

        for slots in range(2, MAXNB + 1, 2):
            pl.when((tally == slots) | (tally == slots - 1))(functools.partial(variant, slots))

    @pl.loop(0, NQB)
    def _(n):
        rows = pl.ds(pl.multiple_of(n * BLK, BLK), BLK)
        for h in range(heads):
            cols = slice(h * HDIM, (h + 1) * HDIM)
            dk_ref[rows, cols] = (acc[h, rows, :HDIM] * scale).astype(jnp.bfloat16)
            dv_ref[rows, cols] = acc[h, rows, HDIM:].astype(jnp.bfloat16)


def attention(links, tallies, q, k, v, g):
    tokens = NQB * BLK
    heads = COLS // HDIM
    spec = pl.BlockSpec(memory_space=pltpu.VMEM)
    smem = pl.BlockSpec(memory_space=pltpu.SMEM)
    flops = heads * NQB * MAXNB * 5 * 2 * BLK**3
    return pl.pallas_call(
        attend,
        out_shape=[jax.ShapeDtypeStruct((tokens, COLS), jnp.bfloat16)] * 3,
        in_specs=[smem, smem] + [spec] * 4,
        out_specs=[spec] * 3,
        scratch_shapes=[
            pltpu.VMEM((heads, 2 * HDIM, 2 * BLK), jnp.bfloat16),
            pltpu.VMEM((heads, NQB, HDIM, BLK), jnp.bfloat16),
            pltpu.VMEM((heads, tokens, 2 * HDIM), jnp.float32),
            pltpu.VMEM((heads, MAXNB, BLK, 2 * BLK), jnp.float32),
        ],
        compiler_params=pltpu.CompilerParams(vmem_limit_bytes=16 << 20),
        cost_estimate=pl.CostEstimate(
            flops=flops, bytes_accessed=7 * tokens * COLS * 2, transcendentals=heads * NQB * MAXNB * BLK * BLK
        ),
    )(links, tallies, q, k, v, g)


def gather_early(layer_rows):
    y = lax.axis_index("dp") // 2
    width = 4 * PIECE
    parts = [
        lax.dynamic_slice_in_dim(layer_rows, turn(y, TURNS[u]) * width, width, 1)
        for u in range(0, EARLY, 2)
    ]
    mine = jnp.concatenate(parts, axis=1)
    whole = lax.all_gather(mine[None], "seq", axis=1, tiled=True)
    return whole.reshape(SIDE, SIDE, BLK, EARLY // 2 * width)


def hand_over(*refs):
    ins, outs, sem = refs[:4], refs[4:8], refs[8]
    copies = [pltpu.make_async_copy(a, b, sem.at[i]) for i, (a, b) in enumerate(zip(ins, outs))]
    for copy in copies:
        copy.start()
    for copy in copies:
        copy.wait()


def settled(arrays):
    return pl.pallas_call(
        hand_over,
        out_shape=[jax.ShapeDtypeStruct(a.shape, a.dtype) for a in arrays],
        in_specs=[pl.BlockSpec(memory_space=pltpu.VMEM)] * 4,
        out_specs=[pl.BlockSpec(memory_space=pltpu.HBM)] * 4,
        scratch_shapes=[pltpu.SemaphoreType.DMA((4,))],
        compiler_params=pltpu.CompilerParams(vmem_limit_bytes=8 << 20),
    )(*arrays)


def local(layer_input, query_rows, key_rows, value_rows, out_grad, neighbours, counts):
    early = gather_early(layer_input[0])
    q, k, v, g = heads_exchange([query_rows[0], key_rows[0], value_rows[0], out_grad[0]])
    dq, dk, dv = attention(neighbours[0], counts[0], q, k, v, g)
    norm_factor = 1.0 / math.sqrt(SEQ * BLK * lax.axis_size("dp"))
    query_grad, key_grad, value_grad, owned = settled(
        closing(norm_factor, layer_input[0], early, dq, dk, dv)
    )
    return query_grad[None], key_grad[None], value_grad[None], owned


def solution(mesh):
    rows = P("dp", "seq", None)
    return jax.shard_map(
        local,
        mesh=mesh,
        in_specs=(rows,) * 5 + (P("dp", None, None), P("dp", None)),
        out_specs=(rows, rows, rows, P(None, "dp", "seq")),
        check_vma=False,
    )
```

```python
import functools
import math

import jax
import jax.numpy as jnp
from jax import lax
from jax.experimental import pallas as pl
from jax.experimental.pallas import tpu as pltpu
from jax.sharding import PartitionSpec as P

HDIM = 128
BLK = 128
MAXNB = 8
NQB = 16
SEQ = 16
SIDE = 4
COLS = 256
LOG2E = 1.4426950408889634
MESH = pl.DeviceIdType.MESH


OFFSETS = (
    (2, 2), (2, 1), (2, 3), (1, 2), (3, 2), (2, 0), (0, 2), (1, 1),
    (3, 3), (1, 3), (3, 1), (1, 0), (3, 0), (0, 1), (0, 3),
)


def peer_of(offset):
    me, core = lax.axis_index("seq"), lax.rem(lax.axis_index("dp"), 2)
    place = []
    for at, step in zip((me // SIDE, lax.rem(me, SIDE)), offset):
        back = (SIDE - step) % SIDE
        place.append(lax.rem(at + step + core * (back - step), SIDE))
    return place[0] * SIDE + place[1]


WINDOW = 1


def block(index, size):
    return pl.ds(pl.multiple_of(index * size, size), size)


def to_heads(*refs):
    ins, outs = refs[:4], refs[4:8]
    send_sem, recv_sem, own_sem = refs[8:]
    me = lax.axis_index("seq")
    barrier = pltpu.get_barrier_semaphore()
    for offset in OFFSETS:
        pl.semaphore_signal(
            barrier, inc=1, device_id={"seq": peer_of(offset)}, device_id_type=MESH
        )
    pl.semaphore_wait(barrier, SEQ - 1)
    groups = []
    for a in range(4):
        if a >= WINDOW:
            for copy in groups[a - WINDOW]:
                copy.wait_send()
        groups.append([])
        for i, offset in enumerate(OFFSETS):
            peer = peer_of(offset)
            copy = pltpu.make_async_remote_copy(
                src_ref=ins[a].at[:, block(peer, COLS)],
                dst_ref=outs[a].at[block(me, BLK), :],
                send_sem=send_sem.at[a, i],
                recv_sem=recv_sem.at[a, i],
                device_id={"seq": peer},
                device_id_type=MESH,
            )
            copy.start()
            groups[a].append(copy)
    owns = []
    for a in range(4):
        own = pltpu.make_async_copy(
            ins[a].at[:, block(me, COLS)], outs[a].at[block(me, BLK), :], own_sem.at[a]
        )
        own.start()
        owns.append(own)
    for group in groups[4 - WINDOW :]:
        for copy in group:
            copy.wait_send()
    for group in groups:
        for copy in group:
            copy.wait_recv()
    for own in owns:
        own.wait()


def heads_exchange(arrays):
    tokens = SEQ * BLK
    return pl.pallas_call(
        to_heads,
        out_shape=[jax.ShapeDtypeStruct((tokens, COLS), jnp.bfloat16)] * 4,
        in_specs=[pl.BlockSpec(memory_space=pltpu.HBM)] * 4,
        out_specs=[pl.BlockSpec(memory_space=pltpu.VMEM)] * 4,
        scratch_shapes=[
            pltpu.SemaphoreType.DMA((4, SEQ - 1)),
            pltpu.SemaphoreType.DMA((4, SEQ - 1)),
            pltpu.SemaphoreType.DMA((4,)),
        ],
        compiler_params=pltpu.CompilerParams(
            collective_id=0, has_side_effects=True, vmem_limit_bytes=58_500_000
        ),
    )(*arrays)


UNITS = 8
EARLY = 4
PIECE = 256
TURNS = (2, 2, 1, 1, 3, 3, 0, 0)
WIDE = 3 * COLS


def turn(at, by):
    return lax.rem(at + by, SIDE)


def finish(norm_factor, x_ref, early_ref, dq_ref, dk_ref, dv_ref, qg_ref, kg_ref, vg_ref, w_ref,
           xg, gt, prod, sib_in, y_out, y_in,
           load_sem, ring_send, ring_recv, back_send, back_recv, own_sem, sib_sem, y_sem):
    me, dp = lax.axis_index("seq"), lax.axis_index("dp")
    x, z, y, core = me // SIDE, lax.rem(me, SIDE), dp // 2, lax.rem(dp, 2)
    f32 = jnp.float32
    grads, homes = (dq_ref, dk_ref, dv_ref), (qg_ref, kg_ref, vg_ref)

    loads = {}
    for u in [*range(EARLY, UNITS), *range(EARLY)]:
        for part in (0, 1):
            spot = part * 2 + u % 2
            cols = slice(part * PIECE, (part + 1) * PIECE)
            if u < EARLY:
                at = (u // 2 * 4 + spot) * PIECE
                source, place = early_ref.at[:, :, :, at : at + PIECE], xg.at[u, :, :, :, cols]
            else:
                source = x_ref.at[:, block(turn(y, TURNS[u]) * 4 + spot, PIECE)]
                place = xg.at[u, x, z, :, cols]
            loads[u, part] = pltpu.make_async_copy(source, place, load_sem.at[u, part])
            loads[u, part].start()
    barrier = pltpu.get_barrier_semaphore()
    friends = [(peer_of(offset), dp) for offset in OFFSETS]
    friends += [(me, y * 2 + 1 - core)]
    friends += [(me, turn(y, by) * 2 + core) for by in (1, 2, 3)]
    for friend in friends:
        pl.semaphore_signal(barrier, inc=1, device_id=friend, device_id_type=MESH)
    pl.semaphore_wait(barrier, len(friends))

    started = []

    def send(src, dst, sems, device):
        copy = pltpu.make_async_remote_copy(
            src_ref=src, dst_ref=dst, send_sem=sems[0], recv_sem=sems[1],
            device_id=device, device_id_type=MESH,
        )
        copy.start()
        started.append(copy)
        return copy

    def ring(u, part, stage):
        cols = slice(part * PIECE, (part + 1) * PIECE)
        along_x = (part == 0) == (stage < 2)
        copies = []
        for way, step in enumerate((1, 3)):
            owner = 0 if stage % 2 == 0 else SIDE - step
            rows = slice(0, BLK) if stage % 2 == 0 else slice(way * (BLK // 2), (way + 1) * (BLK // 2))
            if along_x:
                device = (turn(x, step) * SIDE + z, dp)
                group = (turn(x, owner), z if stage < 2 else slice(None))
            else:
                device = (x * SIDE + turn(z, step), dp)
                group = (x if stage < 2 else slice(None), turn(z, owner))
            place = xg.at[u, group[0], group[1], rows, cols]
            at = (((u - EARLY) * 2 + part) * 4 + stage) * 2 + way
            copies.append(send(place, place, (ring_send.at[at], ring_recv.at[at]), device))
        return copies

    flights = {}

    def advance(u, stage):
        for part in (0, 1):
            if stage == 0:
                loads[u, part].wait()
            else:
                for copy in flights[u, part, stage - 1]:
                    copy.wait_recv()
            if stage < 4:
                flights[u, part, stage] = ring(u, part, stage)

    homeward, owns, siblings, across = [], [], {}, {}

    def go_home(a):
        for i, offset in enumerate(OFFSETS):
            peer = peer_of(offset)
            homeward.append(send(
                grads[a].at[block(peer, BLK), :], homes[a].at[:, block(me, COLS)],
                (back_send.at[a, i], back_recv.at[a, i]), (peer, dp),
            ))
        own = pltpu.make_async_copy(
            grads[a].at[block(me, BLK), :], homes[a].at[:, block(me, COLS)], own_sem.at[a]
        )
        own.start()
        owns.append(own)

    def product(u):
        @pl.loop(0, 2)
        def _(half):
            cols = block(lax.rem(1 - core + half, 2), PIECE)
            right = xg[u, :, :, :, cols].reshape(SEQ * BLK, PIECE)
            prod[u, half] = jnp.dot(gt[...], right, preferred_element_type=f32).astype(jnp.bfloat16)

        siblings[u] = send(
            prod.at[u, 0], sib_in.at[u], (sib_sem.at[0, u], sib_sem.at[1, u]),
            (me, y * 2 + 1 - core),
        )

    def settle(u):
        siblings[u].wait_recv()
        total = prod[u, 1].astype(f32) + sib_in[u].astype(f32)
        if u < UNITS - 2:
            y_out[u] = total.astype(jnp.bfloat16)
            across[u] = send(
                y_out.at[u], y_in.at[u], (y_sem.at[0, u], y_sem.at[1, u]),
                (me, turn(y, TURNS[u]) * 2 + core),
            )
        else:
            for i in range(u % 2, UNITS - 2, 2):
                across[i].wait_recv()
                total += y_in[i].astype(f32)
            for a in range(3):
                for h in range(2):
                    rows = slice(a * COLS + h * HDIM, a * COLS + (h + 1) * HDIM)
                    w_ref[a, (u % 2) * PIECE : (u % 2 + 1) * PIECE, h * HDIM : (h + 1) * HDIM] = (
                        total[rows].T * norm_factor
                    )

    late = range(EARLY, UNITS)
    for u in late:
        advance(u, 0)
    go_home(0)
    for u in late:
        advance(u, 1)
    for u in late:
        advance(u, 2)

    @pl.loop(0, SEQ)
    def _(n):
        for a in range(3):
            for h in range(2):
                tile = grads[a][block(n, BLK), h * HDIM : (h + 1) * HDIM]
                gt[a * COLS + h * HDIM : a * COLS + (h + 1) * HDIM, block(n, BLK)] = tile.T

    ahead, leaving = EARLY, True
    for u in range(EARLY):
        for part in (0, 1):
            loads[u, part].wait()
        product(u)
        advance(ahead, 3)
        ahead += 1
        if u:
            settle(u - 1)
        if u == min(2, EARLY - 1):
            go_home(1)
    settle(EARLY - 1)
    for u in late:
        if ahead < UNITS:
            advance(ahead, 3)
            ahead += 1
        advance(u, 4)
        product(u)
        settle(u)
        if leaving and ahead == UNITS:
            go_home(2)
            leaving = False
    for copy in homeward:
        copy.wait_recv()
    for own in owns:
        own.wait()
    for copy in started:
        copy.wait_send()


def closing(norm_factor, layer_rows, early, dq, dk, dv):
    tokens, width = SEQ * BLK, layer_rows.shape[1]
    vmem, hbm = pl.BlockSpec(memory_space=pltpu.VMEM), pl.BlockSpec(memory_space=pltpu.HBM)
    bf16, f32 = jnp.bfloat16, jnp.float32
    rings = (UNITS - EARLY) * 16
    return pl.pallas_call(
        functools.partial(finish, norm_factor),
        out_shape=[jax.ShapeDtypeStruct((BLK, width), bf16)] * 3
        + [jax.ShapeDtypeStruct((3, 2 * PIECE, COLS), f32)],
        in_specs=[hbm, hbm, vmem, vmem, vmem],
        out_specs=[vmem] * 4,
        scratch_shapes=[
            pltpu.VMEM((UNITS, SIDE, SIDE, BLK, 2 * PIECE), bf16),
            pltpu.VMEM((WIDE, tokens), bf16),
            pltpu.VMEM((UNITS, 2, WIDE, PIECE), bf16),
            pltpu.VMEM((UNITS, WIDE, PIECE), bf16),
            pltpu.VMEM((UNITS - 2, WIDE, PIECE), bf16),
            pltpu.VMEM((UNITS - 2, WIDE, PIECE), bf16),
            pltpu.SemaphoreType.DMA((UNITS, 2)),
            pltpu.SemaphoreType.DMA((rings,)),
            pltpu.SemaphoreType.DMA((rings,)),
            pltpu.SemaphoreType.DMA((3, SEQ - 1)),
            pltpu.SemaphoreType.DMA((3, SEQ - 1)),
            pltpu.SemaphoreType.DMA((3,)),
            pltpu.SemaphoreType.DMA((2, UNITS)),
            pltpu.SemaphoreType.DMA((2, UNITS - 2)),
        ],
        compiler_params=pltpu.CompilerParams(
            collective_id=1, has_side_effects=True, vmem_limit_bytes=40 << 20
        ),
    )(layer_rows, early, dq, dk, dv)


def attend(kv_links, tallies, q_hbm, k_hbm, v_hbm, g_hbm, dq_ref, dk_ref, dv_ref,
           q_ref, k_ref, v_ref, g_ref, wq, turned, acc, sp, sem):
    scale = HDIM ** (-0.5)
    heads = COLS // HDIM
    f32 = jnp.float32
    pairs = ((k_hbm, k_ref), (q_hbm, q_ref), (v_hbm, v_ref), (g_hbm, g_ref))
    loads = [pltpu.make_async_copy(a, b, sem.at[i]) for i, (a, b) in enumerate(pairs)]
    for load in loads:
        load.start()
    acc[...] = jnp.zeros_like(acc)
    wq[...] = jnp.zeros_like(wq)
    loads[0].wait()

    @pl.loop(0, NQB)
    def _(n):
        rows = pl.ds(pl.multiple_of(n * BLK, BLK), BLK)
        for h in range(heads):
            turned[h, n] = k_ref[rows, h * HDIM : (h + 1) * HDIM].astype(f32).T.astype(jnp.bfloat16)

    for load in loads[1:]:
        load.wait()

    @pl.loop(0, NQB)
    def _(b):
        mine = pl.ds(pl.multiple_of(b * BLK, BLK), BLK)
        tally = tallies[b]

        def variant(slots):
            spans = [slice(h * HDIM, (h + 1) * HDIM) for h in range(heads)]
            rows = [block(kv_links[b, j], BLK) for j in range(slots)]
            for h in range(heads):
                wq[h, :HDIM, :HDIM] = q_ref[mine, spans[h]]
                wq[h, HDIM:, HDIM:] = g_ref[mine, spans[h]]
            tops = [None] * heads
            for j in range(slots):
                for h in range(heads):
                    kv = jnp.concatenate([k_ref[rows[j], spans[h]], v_ref[rows[j], spans[h]]], axis=1)
                    pair = lax.dot_general(
                        kv, wq[h], (((1,), (1,)), ((), ())), preferred_element_type=f32
                    )
                    score = pair[:, :HDIM]
                    if j == slots - 1 and slots > 1:
                        score = jnp.where(j < tally, score, -jnp.inf)
                    sp[h, j, :, :HDIM] = score
                    sp[h, j, :, HDIM:] = pair[:, HDIM:]
                    here = jnp.max(score.reshape(BLK // 8, 8, BLK), axis=0)
                    tops[h] = here if j == 0 else jnp.maximum(tops[h], here)
            tops = [jnp.max(top, axis=0, keepdims=True) for top in tops]
            totals, dots = [0.0] * heads, [0.0] * heads
            for j in range(slots):
                for h in range(heads):
                    weight = jnp.exp2((sp[h, j, :, :HDIM] - tops[h]) * (scale * LOG2E))
                    sp[h, j, :, :HDIM] = weight
                    totals[h] += jnp.sum(weight.reshape(BLK // 8, 8, BLK), axis=0)
                    slopes = weight * sp[h, j, :, HDIM:]
                    dots[h] += jnp.sum(slopes.reshape(BLK // 8, 8, BLK), axis=0)
            inverses = [1.0 / jnp.sum(total, axis=0, keepdims=True) for total in totals]
            dots = [jnp.sum(dot, axis=0, keepdims=True) * inv for dot, inv in zip(dots, inverses)]
            dqs = [0.0] * heads
            for j in range(slots):
                for h in range(heads):
                    prob = sp[h, j, :, :HDIM] * inverses[h]
                    slope = (prob * (sp[h, j, :, HDIM:] - dots[h])).astype(jnp.bfloat16)
                    left = jnp.concatenate([slope, prob.astype(jnp.bfloat16)], axis=1)
                    acc[h, rows[j], :] += jnp.dot(left, wq[h], preferred_element_type=f32)
                    dqs[h] += jnp.dot(turned[h, kv_links[b, j]], slope, preferred_element_type=f32)
            for h in range(heads):
                dq_ref[mine, spans[h]] = (dqs[h].T * scale).astype(jnp.bfloat16)

        for slots in range(2, MAXNB + 1, 2):
            pl.when((tally == slots) | (tally == slots - 1))(functools.partial(variant, slots))

    @pl.loop(0, NQB)
    def _(n):
        rows = pl.ds(pl.multiple_of(n * BLK, BLK), BLK)
        for h in range(heads):
            cols = slice(h * HDIM, (h + 1) * HDIM)
            dk_ref[rows, cols] = (acc[h, rows, :HDIM] * scale).astype(jnp.bfloat16)
            dv_ref[rows, cols] = acc[h, rows, HDIM:].astype(jnp.bfloat16)


def attention(links, tallies, q, k, v, g):
    tokens = NQB * BLK
    heads = COLS // HDIM
    spec = pl.BlockSpec(memory_space=pltpu.VMEM)
    smem = pl.BlockSpec(memory_space=pltpu.SMEM)
    flops = heads * NQB * MAXNB * 5 * 2 * BLK**3
    return pl.pallas_call(
        attend,
        out_shape=[jax.ShapeDtypeStruct((tokens, COLS), jnp.bfloat16)] * 3,
        in_specs=[smem, smem] + [pl.BlockSpec(memory_space=pltpu.HBM)] * 4,
        out_specs=[spec] * 3,
        scratch_shapes=[pltpu.VMEM((tokens, COLS), jnp.bfloat16)] * 4
        + [
            pltpu.VMEM((heads, 2 * HDIM, 2 * BLK), jnp.bfloat16),
            pltpu.VMEM((heads, NQB, HDIM, BLK), jnp.bfloat16),
            pltpu.VMEM((heads, tokens, 2 * HDIM), jnp.float32),
            pltpu.VMEM((heads, MAXNB, BLK, 2 * BLK), jnp.float32),
            pltpu.SemaphoreType.DMA((4,)),
        ],
        compiler_params=pltpu.CompilerParams(vmem_limit_bytes=56 << 20),
        cost_estimate=pl.CostEstimate(
            flops=flops, bytes_accessed=7 * tokens * COLS * 2, transcendentals=heads * NQB * MAXNB * BLK * BLK
        ),
    )(links, tallies, q, k, v, g)


def gather_early(layer_rows):
    y = lax.axis_index("dp") // 2
    width = 4 * PIECE
    parts = [
        lax.dynamic_slice_in_dim(layer_rows, turn(y, TURNS[u]) * width, width, 1)
        for u in range(0, EARLY, 2)
    ]
    mine = jnp.concatenate(parts, axis=1)
    whole = lax.all_gather(mine[None], "seq", axis=1, tiled=True)
    return whole.reshape(SIDE, SIDE, BLK, EARLY // 2 * width)


def hand_over(*refs):
    ins, outs, sem = refs[:4], refs[4:8], refs[8]
    copies = [pltpu.make_async_copy(a, b, sem.at[i]) for i, (a, b) in enumerate(zip(ins, outs))]
    for copy in copies:
        copy.start()
    for copy in copies:
        copy.wait()


def settled(arrays):
    return pl.pallas_call(
        hand_over,
        out_shape=[jax.ShapeDtypeStruct(a.shape, a.dtype) for a in arrays],
        in_specs=[pl.BlockSpec(memory_space=pltpu.VMEM)] * 4,
        out_specs=[pl.BlockSpec(memory_space=pltpu.HBM)] * 4,
        scratch_shapes=[pltpu.SemaphoreType.DMA((4,))],
        compiler_params=pltpu.CompilerParams(vmem_limit_bytes=8 << 20),
    )(*arrays)


def local(layer_input, query_rows, key_rows, value_rows, out_grad, neighbours, counts):
    early = gather_early(layer_input[0])
    q, k, v, g = heads_exchange([query_rows[0], key_rows[0], value_rows[0], out_grad[0]])
    dq, dk, dv = attention(neighbours[0], counts[0], q, k, v, g)
    norm_factor = 1.0 / math.sqrt(SEQ * BLK * lax.axis_size("dp"))
    query_grad, key_grad, value_grad, owned = settled(
        closing(norm_factor, layer_input[0], early, dq, dk, dv)
    )
    return query_grad[None], key_grad[None], value_grad[None], owned


def solution(mesh):
    rows = P("dp", "seq", None)
    return jax.shard_map(
        local,
        mesh=mesh,
        in_specs=(rows,) * 5 + (P("dp", None, None), P("dp", None)),
        out_specs=(rows, rows, rows, P(None, "dp", "seq")),
        check_vma=False,
    )
```
